128 devices in a mesh: seq: 32 (over z, x, core), doc: 4 (over y).
Axes of the slice: x: 4, y: 4, z: 4, core: 2. Of those that a mesh axis runs over, the one named last changes fastest.
Arguments:
- values: bfloat16 [4, 8192, 4096], P('doc', 'seq'), may hold values from -6 to 6
- b_in: bfloat16 [4, 8192, 128], P('doc', 'seq'), may hold values from -0.032958984 to 0.032958984
- c_in: bfloat16 [4, 8192, 128], P('doc', 'seq'), may hold values from -6 to 6
- log_decay: float32 [4, 64, 8192], P('doc', None, 'seq'), may hold values from -1 to 0, as said below
- skip: float32 [64], replicated, may hold values from 0.5 to 1.5
- owner: int32 [4, 64], P(None, 'seq'), may hold values from -1 to 3, as said below
Outputs:
- owned: bfloat16 [4, 256, 128, 4096], P('doc', 'seq')
The draws below stay inside these ranges and needn't reach their ends.
Inputs may be any that keep to these rules, and one draw needn't show every extreme that they name: `log_decay`: all entries are at most 0. In each head the per-token rates vary from token to token and from shard to shard. Within each shard of 2 blocks of a document, both blocks name the same owner (so no block is marked -1); in general -1 marks a block that is not kept.
All inputs are finite; a program needn't handle non-finite values.
Results may differ from the reference program's by a relative error of at most 0.0063.
Values may be sent and summed in bfloat16 or wider, within the bound.
No kernel may reach another device: no remote copies, remote signals or barrier semaphores. Data moves between devices by JAX's collectives and lax.ppermute only.
A program may use at most 192 MiB of HBM per device.

```python
import functools
import jax
import jax.numpy as jnp
from jax import lax

HEADS = 64
HDIM = 64
NSTATE = 128
Q = 128
CAP = 2
L_DEV = 256
BLK_DEV = 2
TEXT_NUMBER = 4
WORDS_IN_TEXT = 8192
BLOCKS = 64
N_SEQ = 32


def draw_log_decay(key, part):
    random_seed_chain = jax.random.split(jax.random.fold_in(key, 7), 5)
    shard_count = WORDS_IN_TEXT // L_DEV
    slow_share = 0.5
    lagging_channels = jax.random.uniform(random_seed_chain[0], (TEXT_NUMBER, HEADS, 1)) < slow_share
    factor_each_slice = jnp.exp(jax.random.uniform(random_seed_chain[1], (TEXT_NUMBER, HEADS, shard_count), minval=-0.7, maxval=0.7))
    factor_each_slice = jnp.repeat(factor_each_slice, L_DEV, axis=2)
    noise_amplitude = jnp.exp(jax.random.uniform(random_seed_chain[2], (TEXT_NUMBER, HEADS, WORDS_IN_TEXT), minval=-0.7, maxval=0.7))
    floor_speed = jnp.where(lagging_channels, 0.3 / WORDS_IN_TEXT, 0.03)
    spike_place = jax.random.randint(random_seed_chain[3], (TEXT_NUMBER, 3), 0, WORDS_IN_TEXT)
    spike_magnitude = jax.random.uniform(random_seed_chain[4], (TEXT_NUMBER, 3), minval=0.22, maxval=0.45)
    word_offsets = jnp.arange(WORDS_IN_TEXT)
    spike_happenings = jnp.sum(jnp.where(word_offsets[None, :, None] == spike_place[:, None, :], spike_magnitude[:, None, :], 0.0), axis=2)
    fading_factors = floor_speed * factor_each_slice * noise_amplitude + jnp.where(lagging_channels, spike_happenings[:, None, :], 0.0)
    return (-fading_factors).astype(jnp.float32)


def draw_owner(key, part):
    random_seed_chain = jax.random.split(jax.random.fold_in(key, 11), 3)
    shard_count = BLOCKS // BLK_DEV
    hot_owner = jax.random.randint(random_seed_chain[0], (TEXT_NUMBER, shard_count, 1), 0, TEXT_NUMBER)
    extra_counts = jax.random.randint(random_seed_chain[1], (TEXT_NUMBER, shard_count, TEXT_NUMBER), 0, CAP + 1)
    rank_ids = jnp.arange(TEXT_NUMBER)
    counts = jnp.where(rank_ids[None, None, :] == 0, CAP, extra_counts)
    slot_ids = jnp.arange(BLK_DEV)
    rank_of = slot_ids // CAP
    within = slot_ids % CAP
    wanted = jnp.take(counts, jnp.minimum(rank_of, TEXT_NUMBER - 1), axis=2)
    usable = (rank_of[None, None, :] < TEXT_NUMBER) & (within[None, None, :] < wanted)
    labels = jnp.where(usable, (hot_owner + rank_of[None, None, :]) % TEXT_NUMBER, -1)
    labels = labels.reshape(TEXT_NUMBER * shard_count, BLK_DEV)
    perm_keys = jax.random.split(random_seed_chain[2], TEXT_NUMBER * shard_count)
    orders = jax.vmap(lambda one_key: jax.random.permutation(one_key, BLK_DEV))(perm_keys)
    shuffled = jnp.take_along_axis(labels, orders, axis=1)
    return shuffled.reshape(TEXT_NUMBER, BLOCKS).astype(jnp.int32)


def levels(key, dims, cuts, smallest, largest):
    level = 1.0
    for position, shards_of in cuts:
        steps = jax.random.uniform(jax.random.fold_in(jax.random.fold_in(key, 6), position), (shards_of,), jnp.float32, smallest / len(cuts), largest / len(cuts))
        level = level * jnp.repeat(jnp.exp(steps), dims[position] // shards_of).reshape((-1,) + (1,) * (len(dims) - 1 - position))
    return level


def scatter_about(key, dims, spread, limit, cuts=(), kind=jnp.bfloat16):
    entries = spread * jax.random.normal(key, dims, jnp.float32)
    if cuts:
        entries = entries * levels(key, dims, cuts, -0.22, 0.18)
    return jnp.clip(entries, -limit, limit).astype(kind)


def setup_inputs(seed: int = 0) -> dict:
    streams_of = jax.random.split(jax.random.key(seed), 7)
    return {
        "values": scatter_about(streams_of[0], (TEXT_NUMBER, WORDS_IN_TEXT, HEADS * HDIM), 1.0, 6.0, ((0, 4), (1, 32))),
        "b_in": scatter_about(streams_of[1], (TEXT_NUMBER, WORDS_IN_TEXT, NSTATE), (1.0 / (NSTATE * L_DEV) ** 0.5), 0.032958984, ((0, 4), (1, 32))),
        "c_in": scatter_about(streams_of[2], (TEXT_NUMBER, WORDS_IN_TEXT, NSTATE), 1.0, 6.0, ((0, 4), (1, 32))),
        "log_decay": draw_log_decay(jax.random.fold_in(streams_of[6], 71), 0),
        "skip": jnp.clip(jax.random.uniform(streams_of[4], (HEADS,), jnp.float32, 0.5, 1.5), 0.5, 1.5),
        "owner": draw_owner(jax.random.fold_in(streams_of[6], 71), 0),
    }


def block_pass(carried, inputs, skip):
    value_block, b_block, c_block, decay_block = inputs
    head_count = decay_block.shape[0]
    row_width = value_block.shape[1]
    head_dim = row_width // head_count
    cum_decay = jnp.cumsum(decay_block, axis=1)
    scores = jnp.dot(c_block, b_block.T, preferred_element_type=jnp.float32)
    row_ids = jnp.arange(Q)
    lower_mask = row_ids[:, None] >= row_ids[None, :]
    decay_gap = cum_decay[:, :, None] - cum_decay[:, None, :]
    weights = jnp.where(lower_mask, scores[None] * jnp.exp(jnp.where(lower_mask, decay_gap, 0.0)), 0.0).astype(jnp.bfloat16)
    weights = lax.optimization_barrier(weights)
    value_heads = value_block.reshape(Q, head_count, head_dim).astype(jnp.float32)
    diagonal = jnp.einsum("hts,shp->thp", weights.astype(jnp.float32), value_heads)
    c_weighted = (c_block.astype(jnp.float32)[None] * jnp.exp(cum_decay)[:, :, None]).astype(jnp.bfloat16)
    enter_state = carried.astype(jnp.bfloat16)
    c_weighted, enter_state = lax.optimization_barrier((c_weighted, enter_state))
    carried_term = jnp.einsum("htn,hnp->thp", c_weighted.astype(jnp.float32), enter_state.astype(jnp.float32))
    out_block = (diagonal + carried_term + skip[None, :, None] * value_heads).reshape(Q, row_width).astype(jnp.bfloat16)
    b_weighted = (b_block.astype(jnp.float32)[None] * jnp.exp(cum_decay[:, -1:] - cum_decay)[:, :, None]).astype(jnp.bfloat16)
    b_weighted = lax.optimization_barrier(b_weighted)
    local_state = jnp.einsum("hsn,shp->hnp", b_weighted.astype(jnp.float32), value_heads)
    new_state = jnp.exp(cum_decay[:, -1])[:, None, None] * carried + local_state
    return new_state, out_block


def reference(values, b_in, c_in, log_decay, skip, owner):
    doc_count = values.shape[0]
    seq_len = values.shape[1]
    row_width = values.shape[2]
    head_count = log_decay.shape[1]
    head_dim = row_width // head_count
    state_dim = b_in.shape[2]
    block_count = seq_len // Q
    shard_blocks = block_count // N_SEQ
    step_fn = functools.partial(block_pass, skip=skip)
    picked_docs = []
    for doc_index in range(doc_count):
        value_rows = values[doc_index].reshape(block_count, Q, row_width)
        b_rows = b_in[doc_index].reshape(block_count, Q, state_dim)
        c_rows = c_in[doc_index].reshape(block_count, Q, state_dim)
        decay_rows = log_decay[doc_index].reshape(head_count, block_count, Q).transpose(1, 0, 2)
        start_state = jnp.zeros((head_count, state_dim, head_dim), jnp.float32)
        final_state, out_blocks = lax.scan(step_fn, start_state, (value_rows, b_rows, c_rows, decay_rows))
        shard_rows = out_blocks.reshape(N_SEQ, shard_blocks, Q, row_width)
        owner_rows = owner[doc_index].reshape(N_SEQ, shard_blocks)
        owner_ids = jnp.arange(doc_count, dtype=jnp.int32)
        matches = (owner_rows[:, None, :] == owner_ids[None, :, None]).astype(jnp.int32)
        ranking = jnp.cumsum(matches, axis=2) - 1
        slot_ids = jnp.arange(CAP, dtype=jnp.int32)
        chosen = (matches[:, :, None, :] > 0) & (ranking[:, :, None, :] == slot_ids[None, None, :, None])
        block_ids = jnp.arange(shard_blocks, dtype=jnp.int32)
        source_index = jnp.sum(jnp.where(chosen, block_ids, 0), axis=3).astype(jnp.int32)
        present = jnp.any(chosen, axis=3)
        shard_ids = jnp.arange(N_SEQ, dtype=jnp.int32)
        picked = shard_rows[shard_ids[:, None, None], source_index]
        picked = jnp.where(present[:, :, :, None, None], picked, jnp.zeros((), picked.dtype))
        picked_docs.append(picked)
    stacked = jnp.stack(picked_docs)
    return stacked.transpose(2, 1, 0, 3, 4, 5).reshape(doc_count, N_SEQ * doc_count * CAP, Q, row_width)
```

```python
import functools

import jax
import jax.numpy as jnp
from jax import lax
from jax.experimental import pallas as pl
from jax.experimental.pallas import tpu as pltpu
from jax.sharding import PartitionSpec as P

Q = 128
ROW = 8
GH = 8
TAIL = 16
F32 = jnp.float32
BF = jnp.bfloat16


def iota(shape, dim):
    return lax.broadcasted_iota(jnp.int32, shape, dim)


def dot(a, b, ca=1, cb=0):
    return lax.dot_general(a, b, (((ca,), (cb,)), ((), ())), preferred_element_type=F32)


def thirds(x):
    hi = x.astype(BF)
    rest = x - hi.astype(F32)
    mid = rest.astype(BF)
    lo = (rest - mid.astype(F32)).astype(BF)
    return hi, mid, lo


def stacked(log_decay):
    hi, mid, lo = thirds(log_decay)
    parts = [hi.astype(F32), mid.astype(F32), lo.astype(F32), jnp.zeros(log_decay.shape, F32)]
    return jnp.concatenate(parts, axis=0).astype(BF)


def triangle(n, strict_upper=False):
    rows, cols = iota((n, n), 0), iota((n, n), 1)
    keep = cols > rows if strict_upper else cols <= rows
    return jnp.where(keep, 1.0, 0.0).astype(BF)


def spread(columns, width):
    n = GH * width
    rows, cols = iota((4 * GH, n), 0), iota((4 * GH, n), 1)
    pick = jnp.where((rows % GH == cols // width) & (rows < 3 * GH), 1.0, 0.0).astype(BF)
    hi, mid, lo = thirds(columns)
    return dot(hi, pick) + dot(mid, pick) + dot(lo, pick)


def states_kernel(place, values, log_decay, b_in, *outs):
    step = pl.program_id(0)
    tokens = values.shape[0]
    parts = stacked(log_decay[...])
    after = spread(dot(triangle(tokens, True), parts, 1, 1), values.shape[1] // GH)
    first = spread(dot(jnp.ones((8, tokens), BF), parts, 1, 1), values.shape[1] // GH)[0:1]
    scaled = (values[...].astype(F32) * jnp.exp(after)).astype(BF)
    state = dot(b_in[...], scaled, 0, 0).astype(BF)
    hi, mid, lo = thirds(first)
    row = iota((TAIL, values.shape[1]), 0)
    tail = jnp.where(row == 0, hi.astype(F32), jnp.where(row == 1, mid.astype(F32), lo.astype(F32)))
    tail = tail.astype(BF)
    for slot, out in enumerate(outs):

        @pl.when(step == slot)
        def _():
            out[0 : state.shape[0], :] = state
            out[state.shape[0] :, :] = tail


def total_of(piece, n):
    tail = piece[n : n + TAIL, :].astype(F32)
    return tail[0:1] + tail[1:2] + tail[2:3]


def row_kernel(place, *refs):
    pieces, out = refs[:-1], refs[-1]
    n = out.shape[0] - TAIL
    me = place[0]
    where = [lax.rem(me - k + ROW, ROW) for k in range(ROW)]
    totals = [total_of(p, n) for p in pieces]
    acc = jnp.zeros((n, out.shape[1]), F32)
    for k in range(ROW):
        later = jnp.zeros_like(totals[0])
        for j in range(ROW):
            if j != k:
                later = later + jnp.where(where[j] > where[k], totals[j], 0.0)
        acc = acc + jnp.exp(later) * pieces[k][0:n, :].astype(F32)
    total = totals[0]
    for j in range(1, ROW):
        total = total + totals[j]
    hi, mid, lo = thirds(total)
    row = iota((TAIL, out.shape[1]), 0)
    tail = jnp.where(row == 0, hi.astype(F32), jnp.where(row == 1, mid.astype(F32), lo.astype(F32)))
    out[0:n, :] = acc.astype(BF)
    out[n:, :] = tail.astype(BF)


def enter_kernel(place, *refs):
    pieces, rows = refs[:ROW], refs[ROW : ROW + 3]
    outs, held, totals, sent = refs[ROW + 3 : 2 * ROW + 3], refs[-3], refs[-2], refs[-1]
    n = outs[0].shape[0]
    me = place[0]
    for k in range(ROW):
        slot = lax.rem(me - k + ROW, ROW)
        held[slot] = pieces[k][0:n, :]
        totals[slot] = jnp.broadcast_to(total_of(pieces[k], n), totals.shape[1:])
    one, two, three = rows
    near = total_of(one, n)
    enter = one[0:n, :].astype(F32)
    enter = enter + jnp.exp(near) * two[0:n, :].astype(F32)
    enter = enter + jnp.exp(near + total_of(two, n)) * three[0:n, :].astype(F32)
    for q in range(ROW):
        sent[lax.rem(q - me + ROW, ROW)] = enter.astype(BF)
        if q + 1 < ROW:
            enter = jnp.exp(totals[q][0:1]) * enter + held[q].astype(F32)
    for k in range(ROW):
        outs[k][...] = sent[k]


def local_kernel(skip, values, log_decay, b_in, c_in, out):
    group = pl.program_id(0)
    tokens, width = values.shape
    hdim = width // GH
    blocks = tokens // Q
    parts = stacked(log_decay[...])
    lower = triangle(tokens)
    columns = spread(dot(lower, parts, 1, 1), Q)
    line = dot(parts, lower, 1, 1)
    line = line[0:GH] + line[GH : 2 * GH] + line[2 * GH : 3 * GH]
    scores = dot(c_in[...], b_in[...], 1, 1)
    keep = iota((Q, Q), 0) >= iota((Q, Q), 1)
    lanes = iota((Q, 2 * hdim), 1) < hdim
    for pair in range(GH // 2):
        col = slice(pair * 2 * hdim, (pair + 1) * 2 * hdim)
        vals = values[:, col]
        halves = [
            [jnp.where(lanes, vals[j * Q : (j + 1) * Q], 0).astype(BF) for j in range(blocks)],
            [jnp.where(lanes, 0, vals[j * Q : (j + 1) * Q]).astype(BF) for j in range(blocks)],
        ]
        first = skip[group * GH + 2 * pair]
        second = skip[group * GH + 2 * pair + 1]
        gain = jnp.where(lanes[0:1], first, second)
        for i in range(blocks):
            left, right = [], []
            for side in range(2):
                head = 2 * pair + side
                for j in range(i + 1):
                    gap = columns[i * Q : (i + 1) * Q, head * Q : (head + 1) * Q]
                    gap = gap - line[head : head + 1, j * Q : (j + 1) * Q]
                    if i == j:
                        gap = jnp.where(keep, gap, -1e30)
                    here = scores[i * Q : (i + 1) * Q, j * Q : (j + 1) * Q]
                    left.append((here * jnp.exp(gap)).astype(BF))
                    right.append(halves[side][j])
            acc = dot(jnp.concatenate(left, axis=1), jnp.concatenate(right, axis=0))
            acc = acc + gain * vals[i * Q : (i + 1) * Q].astype(F32)
            out[i * Q : (i + 1) * Q, col] = acc


def carried_kernel(place, *refs):
    enters, local, log_decay, c_in = refs[:ROW], refs[ROW], refs[ROW + 1], refs[ROW + 2]
    outs, enter = refs[ROW + 3 : -1], refs[-1]
    step = pl.program_id(0)
    for k in range(ROW):

        @pl.when(step == k)
        def _():
            enter[...] = enters[k][...]

    tokens, width = local.shape
    parts = stacked(log_decay[...])
    decay = jnp.exp(spread(dot(triangle(tokens), parts, 1, 1), width // GH))
    whole = local[...] + decay * dot(c_in[...], enter[...])
    for j, out in enumerate(outs):
        out[...] = whole[j * Q : (j + 1) * Q].astype(BF)


def owned_kernel(place, owner, *refs):
    blocks, out, zeros, sems = refs[:-3], refs[-3], refs[-2], refs[-1]
    docs = len(blocks) // 2
    me = place[2]
    zeros[...] = jnp.zeros_like(zeros)
    waits = []
    for r in range(docs):
        doc = lax.rem(me + r, docs)
        first = owner[doc, 0] == me
        second = owner[doc, 1] == me
        plans = (
            (first, jnp.logical_and(jnp.logical_not(first), second)),
            (False, jnp.logical_and(first, second)),
        )
        for k in range(2):
            sem = sems.at[2 * r + k]
            dst = out.at[2 * doc + k]
            from_first, from_second = plans[k]
            if k == 0:

                @pl.when(from_first)
                def _():
                    pltpu.make_async_copy(blocks[2 * r], dst, sem).start()

            @pl.when(from_second)
            def _():
                pltpu.make_async_copy(blocks[2 * r + 1], dst, sem).start()

            @pl.when(jnp.logical_not(jnp.logical_or(from_first, from_second)))
            def _():
                pltpu.make_async_copy(zeros, dst, sem).start()

            waits.append((dst, sem))
    for dst, sem in waits:
        pltpu.make_async_copy(zeros, dst, sem).wait()


def whole_spec(shape):
    return pl.BlockSpec(shape, lambda *_: (0,) * len(shape))


def local(values, b_in, c_in, log_decay, skip, owner):
    seq_n = lax.axis_size("seq")
    doc_n = lax.axis_size("doc")
    levels = seq_n // ROW
    values, b_in, c_in, log_decay = values[0], b_in[0], c_in[0], log_decay[0]
    tokens, width = values.shape
    heads = log_decay.shape[0]
    n = b_in.shape[1]
    groups = heads // GH
    gw = width // groups
    seq_at = lax.axis_index("seq")
    doc_at = lax.axis_index("doc")
    place = jnp.stack([seq_at % ROW, seq_at // ROW, doc_at]).astype(jnp.int32)

    def in_row(x, k):
        pairs = [(z * ROW + q, z * ROW + (q + k) % ROW) for z in range(levels) for q in range(ROW)]
        return lax.ppermute(x, "seq", pairs)

    def down(x, k):
        pairs = [(z * ROW + q, (z + k) * ROW + q) for z in range(levels - k) for q in range(ROW)]
        return lax.ppermute(x, "seq", pairs)

    def over_docs(x, k):
        return lax.ppermute(x, "doc", [(d, (d + k) % doc_n) for d in range(doc_n)])

    piece = jax.ShapeDtypeStruct((n + TAIL, gw), BF)
    pieces = pl.pallas_call(
        states_kernel,
        name="states",
        out_shape=[piece] * ROW,
        grid_spec=pltpu.PrefetchScalarGridSpec(
            num_scalar_prefetch=1,
            grid=(groups,),
            in_specs=[
                pl.BlockSpec((tokens, gw), lambda k, at: (0, lax.rem(at[0] + k, ROW))),
                pl.BlockSpec((GH, tokens), lambda k, at: (lax.rem(at[0] + k, ROW), 0)),
                whole_spec((tokens, n)),
            ],
            out_specs=[whole_spec(piece.shape)] * ROW,
        ),
    )(place, values, log_decay, b_in)
    pieces = [pieces[0]] + [in_row(pieces[k], k) for k in range(1, ROW)]

    local_out = pl.pallas_call(
        local_kernel,
        name="local",
        out_shape=jax.ShapeDtypeStruct((tokens, width), F32),
        grid=(groups,),
        in_specs=[
            pl.BlockSpec(memory_space=pltpu.SMEM),
            pl.BlockSpec((tokens, gw), lambda g: (0, g)),
            pl.BlockSpec((GH, tokens), lambda g: (g, 0)),
            whole_spec((tokens, n)),
            whole_spec((tokens, n)),
        ],
        out_specs=pl.BlockSpec((tokens, gw), lambda g: (0, g)),
    )(skip, values, log_decay, b_in, c_in)

    prefetch = pltpu.PrefetchScalarGridSpec
    row = pl.pallas_call(
        row_kernel,
        name="row",
        out_shape=piece,
        grid_spec=prefetch(
            num_scalar_prefetch=1,
            grid=(1,),
            in_specs=[whole_spec(piece.shape)] * ROW,
            out_specs=whole_spec(piece.shape),
        ),
    )(place, *pieces)
    rows = [down(row, k) for k in (1, 2, 3)]

    enter = jax.ShapeDtypeStruct((n, gw), BF)
    enters = pl.pallas_call(
        enter_kernel,
        name="enter",
        out_shape=[enter] * ROW,
        grid_spec=prefetch(
            num_scalar_prefetch=1,
            grid=(1,),
            in_specs=[whole_spec(piece.shape)] * (ROW + 3),
            out_specs=[whole_spec(enter.shape)] * ROW,
            scratch_shapes=[
                pltpu.VMEM((ROW, n, gw), BF),
                pltpu.VMEM((ROW, 8, gw), F32),
                pltpu.VMEM((ROW, n, gw), BF),
            ],
        ),
    )(place, *pieces, *rows)
    enters = [enters[0]] + [in_row(enters[k], k) for k in range(1, ROW)]

    def from_group(k, at):
        return lax.rem(at[0] - k + ROW, ROW)

    block = jax.ShapeDtypeStruct((Q, width), BF)
    first, second = pl.pallas_call(
        carried_kernel,
        name="carried",
        out_shape=[block] * 2,
        grid_spec=prefetch(
            num_scalar_prefetch=1,
            grid=(groups,),
            in_specs=[whole_spec(enter.shape)] * ROW
            + [
                pl.BlockSpec((tokens, gw), lambda k, at: (0, from_group(k, at))),
                pl.BlockSpec((GH, tokens), lambda k, at: (from_group(k, at), 0)),
                whole_spec((tokens, n)),
            ],
            out_specs=[pl.BlockSpec((Q, gw), lambda k, at: (0, from_group(k, at)))] * 2,
            scratch_shapes=[pltpu.VMEM((n, gw), BF)],
        ),
    )(place, *enters, local_out, log_decay, c_in)

    left_first = over_docs(first, 1)
    right_second = over_docs(second, doc_n - 1)
    left_second = over_docs(second, 1)
    right_first = over_docs(first, doc_n - 1)
    far_first = over_docs(left_first, 1)
    far_second = over_docs(right_second, doc_n - 1)
    blocks = [first, second, right_first, right_second, far_first, far_second, left_first, left_second]

    owned = pl.pallas_call(
        owned_kernel,
        name="owned",
        out_shape=jax.ShapeDtypeStruct((doc_n * 2, Q, width), BF),
        in_specs=[pl.BlockSpec(memory_space=pltpu.SMEM)] * 2
        + [pl.BlockSpec(memory_space=pl.ANY)] * len(blocks),
        out_specs=pl.BlockSpec(memory_space=pl.ANY),
        scratch_shapes=[pltpu.VMEM((Q, width), BF), pltpu.SemaphoreType.DMA((len(blocks),))],
    )(place, owner, *blocks)
    return owned[None]


def solution(mesh):
    in_specs = (
        P("doc", "seq", None),
        P("doc", "seq", None),
        P("doc", "seq", None),
        P("doc", None, "seq"),
        P(),
        P(None, "seq"),
    )
    out_specs = P("doc", "seq", None, None)
    return jax.shard_map(local, mesh=mesh, in_specs=in_specs, out_specs=out_specs, check_vma=False)
```

```python
import jax
import jax.numpy as jnp
from jax import lax
from jax.experimental import pallas as pl
from jax.experimental.pallas import tpu as pltpu
from jax.sharding import PartitionSpec as P

Q = 128
ROW = 8
GH = 8
TAIL = 16
F32 = jnp.float32
BF = jnp.bfloat16


def iota(shape, dim):
    return lax.broadcasted_iota(jnp.int32, shape, dim)


def dot(a, b, ca=1, cb=0):
    return lax.dot_general(a, b, (((ca,), (cb,)), ((), ())), preferred_element_type=F32)


def thirds(x):
    hi = x.astype(BF)
    rest = x - hi.astype(F32)
    mid = rest.astype(BF)
    lo = (rest - mid.astype(F32)).astype(BF)
    return hi, mid, lo


def triangle(n, strict_upper=False):
    rows, cols = iota((n, n), 0), iota((n, n), 1)
    keep = cols > rows if strict_upper else cols <= rows
    return jnp.where(keep, 1.0, 0.0).astype(BF)


def summed(weights, log_decay):
    heads = log_decay.shape[0]
    parts = jnp.concatenate([p.astype(F32) for p in thirds(log_decay)], axis=0).astype(BF)
    sums = dot(weights, parts, 1, 1)
    return sums[:, 0:heads] + sums[:, heads : 2 * heads] + sums[:, 2 * heads : 3 * heads]


def coded(sums):
    return jnp.concatenate([p.astype(F32) for p in thirds(sums)], axis=1).astype(BF)


def spread(code, first_head, heads, width, count):
    shape = (3 * heads, count * width)
    head = jnp.bitwise_and(iota(shape, 0), heads - 1)
    want = lax.shift_right_logical(iota(shape, 1), width.bit_length() - 1) + first_head
    return dot(code, jnp.where(head == want, 1.0, 0.0).astype(BF))


def states_kernel(place, values, log_decay, b_in, *refs):
    outs, cum, code, sent = refs[:ROW], refs[ROW], refs[ROW + 1], refs[ROW + 2]
    step = pl.program_id(0)
    tokens, width = values.shape
    heads = log_decay.shape[0]
    n = b_in.shape[1]
    hdim = outs[0].shape[1] // GH
    per_step = width // outs[0].shape[1]

    @pl.when(step == 0)
    def _():
        code[0:tokens, :] = coded(summed(triangle(tokens, True), log_decay[...]))
        code[tokens:, :] = coded(summed(jnp.ones((TAIL, tokens), BF), log_decay[...]))
        cum[...] = coded(summed(triangle(tokens), log_decay[...]))

    for i in range(per_step):
        group = step * per_step + i
        lanes = slice(i * GH * hdim, (i + 1) * GH * hdim)
        wide = spread(code[...], group * GH, heads, hdim, GH)
        scaled = (values[:, lanes].astype(F32) * jnp.exp(wide[0:tokens])).astype(BF)
        slot = lax.rem(group - place[0] + ROW, ROW)
        sent[slot, 0:n, :] = dot(b_in[...], scaled, 0, 0).astype(BF)
        sent[slot, n:, :] = tail_of(wide[tokens : tokens + 1])

    @pl.when(step == pl.num_programs(0) - 1)
    def _():
        for k, out in enumerate(outs):
            out[...] = sent[k]


def tail_of(total):
    hi, mid, lo = thirds(total)
    row = iota((TAIL, total.shape[1]), 0)
    tail = jnp.where(row == 0, hi.astype(F32), jnp.where(row == 1, mid.astype(F32), lo.astype(F32)))
    return tail.astype(BF)


def total_of(piece, n):
    tail = piece[n : n + TAIL, :].astype(F32)
    return tail[0:1] + tail[1:2] + tail[2:3]


def row_kernel(place, *refs):
    pieces, out = refs[:-1], refs[-1]
    n = out.shape[0] - TAIL
    me = place[0]
    where = [lax.rem(me - k + ROW, ROW) for k in range(ROW)]
    totals = [total_of(p, n) for p in pieces]
    acc = jnp.zeros((n, out.shape[1]), F32)
    for k in range(ROW):
        later = jnp.zeros_like(totals[0])
        for j in range(ROW):
            if j != k:
                later = later + jnp.where(where[j] > where[k], totals[j], 0.0)
        acc = acc + jnp.exp(later) * pieces[k][0:n, :].astype(F32)
    total = totals[0]
    for j in range(1, ROW):
        total = total + totals[j]
    out[0:n, :] = acc.astype(BF)
    out[n:, :] = tail_of(total)


def enter_kernel(place, *refs):
    pieces, rows = refs[:ROW], refs[ROW : ROW + 3]
    outs, held, totals, sent = refs[ROW + 3 : 2 * ROW + 3], refs[-3], refs[-2], refs[-1]
    n = outs[0].shape[0]
    me = place[0]
    for k in range(ROW):
        slot = lax.rem(me - k + ROW, ROW)
        held[slot] = pieces[k][0:n, :]
        totals[slot] = jnp.broadcast_to(total_of(pieces[k], n), totals.shape[1:])
    one, two, three = rows
    near = total_of(one, n)
    enter = one[0:n, :].astype(F32)
    enter = enter + jnp.exp(near) * two[0:n, :].astype(F32)
    enter = enter + jnp.exp(near + total_of(two, n)) * three[0:n, :].astype(F32)
    for q in range(ROW):
        sent[lax.rem(q - me + ROW, ROW)] = enter.astype(BF)
        if q + 1 < ROW:
            enter = jnp.exp(totals[q][0:1]) * enter + held[q].astype(F32)
    for k in range(ROW):
        outs[k][...] = sent[k]


def local_kernel(skip, values, log_decay, cum, b_in, c_in, out):
    group = pl.program_id(0)
    tokens, width = values.shape
    hdim = width // GH
    blocks = tokens // Q
    columns = spread(cum[...], group * GH, cum.shape[1] // 3, Q, GH)
    parts = jnp.concatenate([p.astype(F32) for p in thirds(log_decay[...])], axis=0).astype(BF)
    line = dot(parts, triangle(tokens), 1, 1)
    line = line[0:GH] + line[GH : 2 * GH] + line[2 * GH : 3 * GH]
    scores = dot(c_in[...], b_in[...], 1, 1)
    keep = iota((Q, Q), 0) >= iota((Q, Q), 1)
    lanes = iota((Q, 2 * hdim), 1) < hdim
    for pair in range(GH // 2):
        col = slice(pair * 2 * hdim, (pair + 1) * 2 * hdim)
        vals = values[:, col]
        halves = [
            [jnp.where(lanes, vals[j * Q : (j + 1) * Q], 0).astype(BF) for j in range(blocks)],
            [jnp.where(lanes, 0, vals[j * Q : (j + 1) * Q]).astype(BF) for j in range(blocks)],
        ]
        first = skip[group * GH + 2 * pair]
        second = skip[group * GH + 2 * pair + 1]
        gain = jnp.where(lanes[0:1], first, second)
        for i in range(blocks):
            left, right = [], []
            for side in range(2):
                head = 2 * pair + side
                for j in range(i + 1):
                    gap = columns[i * Q : (i + 1) * Q, head * Q : (head + 1) * Q]
                    gap = gap - line[head : head + 1, j * Q : (j + 1) * Q]
                    if i == j:
                        gap = jnp.where(keep, gap, -1e30)
                    here = scores[i * Q : (i + 1) * Q, j * Q : (j + 1) * Q]
                    left.append((here * jnp.exp(gap)).astype(BF))
                    right.append(halves[side][j])
            acc = dot(jnp.concatenate(left, axis=1), jnp.concatenate(right, axis=0))
            acc = acc + gain * vals[i * Q : (i + 1) * Q].astype(F32)
            out[i * Q : (i + 1) * Q, col] = acc


def carried_kernel(place, *refs):
    enters, local, cum, c_in = refs[:ROW], refs[ROW], refs[ROW + 1], refs[ROW + 2]
    outs, enter = refs[ROW + 3 : -1], refs[-1]
    step = pl.program_id(0)
    gw = enters[0].shape[1]

    @pl.when(step == 0)
    def _():
        for k in range(ROW):
            enter[lax.rem(place[0] - k + ROW, ROW)] = enters[k][...]

    per_step = local.shape[1] // gw
    heads = cum.shape[1] // 3
    for i in range(per_step):
        group = step * per_step + i
        lanes = slice(i * gw, (i + 1) * gw)
        decay = jnp.exp(spread(cum[...], group * GH, heads, gw // GH, GH))
        whole = local[:, lanes] + decay * dot(c_in[...], enter[group])
        for j, out in enumerate(outs):
            out[:, lanes] = whole[j * Q : (j + 1) * Q].astype(BF)


def owned_kernel(place, owner, *refs):
    blocks, out, held, zeros, into, away = refs[:-5], refs[-5], refs[-4], refs[-3], refs[-2], refs[-1]
    docs = len(blocks) // 2
    me = place[2]
    plans = []
    for r in range(docs):
        doc = lax.rem(me + r, docs)
        first = owner[doc, 0] == me
        second = owner[doc, 1] == me
        plans.append((2 * r, 2 * doc, first, jnp.logical_and(jnp.logical_not(first), second)))
        plans.append((2 * r, 2 * doc + 1, None, jnp.logical_and(first, second)))

    def read(source, i):
        return pltpu.make_async_copy(blocks[source], held.at[i], into.at[i])

    def write(source, i, to):
        return pltpu.make_async_copy(source, out.at[to], away.at[i])

    for i, (source, to, from_first, from_second) in enumerate(plans):
        if from_first is not None:

            @pl.when(from_first)
            def _():
                read(source, i).start()

        @pl.when(from_second)
        def _():
            read(source + 1, i).start()

    zeros[...] = jnp.zeros_like(zeros)
    for i, (source, to, from_first, from_second) in enumerate(plans):
        some = from_second if from_first is None else jnp.logical_or(from_first, from_second)

        @pl.when(jnp.logical_not(some))
        def _():
            write(zeros, i, to).start()

    for i, (source, to, from_first, from_second) in enumerate(plans):
        some = from_second if from_first is None else jnp.logical_or(from_first, from_second)

        @pl.when(some)
        def _():
            read(source, i).wait()
            write(held.at[i], i, to).start()

    for i, (source, to, from_first, from_second) in enumerate(plans):
        write(zeros, i, to).wait()


def whole_spec(shape):
    return pl.BlockSpec(shape, lambda *_: (0,) * len(shape))


def local(values, b_in, c_in, log_decay, skip, owner):
    seq_n = lax.axis_size("seq")
    doc_n = lax.axis_size("doc")
    levels = seq_n // ROW
    values, b_in, c_in, log_decay = values[0], b_in[0], c_in[0], log_decay[0]
    tokens, width = values.shape
    heads = log_decay.shape[0]
    n = b_in.shape[1]
    groups = heads // GH
    gw = width // groups
    seq_at = lax.axis_index("seq")
    doc_at = lax.axis_index("doc")
    place = jnp.stack([seq_at % ROW, seq_at // ROW, doc_at]).astype(jnp.int32)

    def in_row(x, k):
        pairs = [(z * ROW + q, z * ROW + (q + k) % ROW) for z in range(levels) for q in range(ROW)]
        return lax.ppermute(x, "seq", pairs)

    def down(x, k):
        pairs = [(z * ROW + q, (z + k) * ROW + q) for z in range(levels - k) for q in range(ROW)]
        return lax.ppermute(x, "seq", pairs)

    def over_docs(x, k):
        return lax.ppermute(x, "doc", [(d, (d + k) % doc_n) for d in range(doc_n)])

    piece = jax.ShapeDtypeStruct((n + TAIL, gw), BF)
    code = jax.ShapeDtypeStruct((tokens, 3 * heads), BF)
    steps = 4
    wide = width // steps
    *pieces, cum = pl.pallas_call(
        states_kernel,
        name="states",
        out_shape=[piece] * ROW + [code],
        grid_spec=pltpu.PrefetchScalarGridSpec(
            num_scalar_prefetch=1,
            grid=(steps,),
            in_specs=[
                pl.BlockSpec((tokens, wide), lambda k, at: (0, k)),
                whole_spec((heads, tokens)),
                whole_spec((tokens, n)),
            ],
            out_specs=[whole_spec(piece.shape)] * ROW + [whole_spec(code.shape)],
            scratch_shapes=[
                pltpu.VMEM((tokens + TAIL, 3 * heads), BF),
                pltpu.VMEM((ROW,) + piece.shape, BF),
            ],
        ),
    )(place, values, log_decay, b_in)
    pieces = [pieces[0]] + [in_row(pieces[k], k) for k in range(1, ROW)]

    local_out = pl.pallas_call(
        local_kernel,
        name="local",
        out_shape=jax.ShapeDtypeStruct((tokens, width), F32),
        grid=(groups,),
        in_specs=[
            pl.BlockSpec(memory_space=pltpu.SMEM),
            pl.BlockSpec((tokens, gw), lambda g: (0, g)),
            pl.BlockSpec((GH, tokens), lambda g: (g, 0)),
            whole_spec(code.shape),
            whole_spec((tokens, n)),
            whole_spec((tokens, n)),
        ],
        out_specs=pl.BlockSpec((tokens, gw), lambda g: (0, g)),
    )(skip, values, log_decay, cum, b_in, c_in)

    smem = pl.BlockSpec(memory_space=pltpu.SMEM)
    vmem = pl.BlockSpec(memory_space=pltpu.VMEM)
    row = pl.pallas_call(
        row_kernel, name="row", out_shape=piece, in_specs=[smem] + [vmem] * ROW, out_specs=vmem
    )(place, *pieces)
    rows = [down(row, k) for k in (1, 2, 3)]

    enter = jax.ShapeDtypeStruct((n, gw), BF)
    enters = pl.pallas_call(
        enter_kernel,
        name="enter",
        out_shape=[enter] * ROW,
        in_specs=[smem] + [vmem] * (ROW + 3),
        out_specs=[vmem] * ROW,
        scratch_shapes=[
            pltpu.VMEM((ROW, n, gw), BF),
            pltpu.VMEM((ROW, 8, gw), F32),
            pltpu.VMEM((ROW, n, gw), BF),
        ],
    )(place, *pieces, *rows)
    enters = [enters[0]] + [in_row(enters[k], k) for k in range(1, ROW)]

    block = jax.ShapeDtypeStruct((Q, width), BF)
    first, second = pl.pallas_call(
        carried_kernel,
        name="carried",
        out_shape=[block] * 2,
        grid_spec=pltpu.PrefetchScalarGridSpec(
            num_scalar_prefetch=1,
            grid=(steps,),
            in_specs=[whole_spec(enter.shape)] * ROW
            + [
                pl.BlockSpec((tokens, wide), lambda k, at: (0, k)),
                whole_spec(code.shape),
                whole_spec((tokens, n)),
            ],
            out_specs=[pl.BlockSpec((Q, wide), lambda k, at: (0, k))] * 2,
            scratch_shapes=[pltpu.VMEM((ROW, n, gw), BF)],
        ),
    )(place, *enters, local_out, cum, c_in)

    left_first = over_docs(first, 1)
    right_second = over_docs(second, doc_n - 1)
    left_second = over_docs(second, 1)
    right_first = over_docs(first, doc_n - 1)
    far_first = over_docs(left_first, 1)
    far_second = over_docs(right_second, doc_n - 1)
    blocks = [first, second, right_first, right_second, far_first, far_second, left_first, left_second]

    owned = pl.pallas_call(
        owned_kernel,
        name="owned",
        out_shape=jax.ShapeDtypeStruct((doc_n * 2, Q, width), BF),
        in_specs=[pl.BlockSpec(memory_space=pltpu.SMEM)] * 2
        + [pl.BlockSpec(memory_space=pl.ANY)] * len(blocks),
        out_specs=pl.BlockSpec(memory_space=pl.ANY),
        scratch_shapes=[
            pltpu.VMEM((len(blocks), Q, width), BF),
            pltpu.VMEM((Q, width), BF),
            pltpu.SemaphoreType.DMA((len(blocks),)),
            pltpu.SemaphoreType.DMA((len(blocks),)),
        ],
    )(place, owner, *blocks)
    return owned[None]


def solution(mesh):
    in_specs = (
        P("doc", "seq", None),
        P("doc", "seq", None),
        P("doc", "seq", None),
        P("doc", None, "seq"),
        P(),
        P(None, "seq"),
    )
    out_specs = P("doc", "seq", None, None)
    return jax.shard_map(local, mesh=mesh, in_specs=in_specs, out_specs=out_specs, check_vma=False)
```

```python
import functools

import jax
import jax.numpy as jnp
from jax import lax
from jax.experimental import pallas as pl
from jax.experimental.pallas import tpu as pltpu
from jax.sharding import PartitionSpec as P

Q = 128
ROW = 4
CORES = 2
GH = 8
HDIM = 64
WIDE = 1024
EARLY = (16, 24)
TAIL = 16
F32 = jnp.float32
BF = jnp.bfloat16


def iota(shape, dim):
    return lax.broadcasted_iota(jnp.int32, shape, dim)


def dot(a, b, ca=1, cb=0):
    return lax.dot_general(a, b, (((ca,), (cb,)), ((), ())), preferred_element_type=F32)


def thirds(x):
    hi = x.astype(BF)
    rest = x - hi.astype(F32)
    mid = rest.astype(BF)
    lo = (rest - mid.astype(F32)).astype(BF)
    return hi, mid, lo


def triangle(n, strict_upper=False):
    rows, cols = iota((n, n), 0), iota((n, n), 1)
    keep = cols > rows if strict_upper else cols <= rows
    return jnp.where(keep, 1.0, 0.0).astype(BF)


def summed(weights, log_decay):
    heads = log_decay.shape[0]
    parts = jnp.concatenate([p.astype(F32) for p in thirds(log_decay)], axis=0).astype(BF)
    sums = dot(weights, parts, 1, 1)
    return sums[:, 0:heads] + sums[:, heads : 2 * heads] + sums[:, 2 * heads : 3 * heads]


def coded(sums):
    return jnp.concatenate([p.astype(F32) for p in thirds(sums)], axis=1).astype(BF)


def spread(code, first_head, heads, width, count):
    shape = (3 * heads, count * width)
    head = jnp.bitwise_and(iota(shape, 0), heads - 1)
    want = lax.shift_right_logical(iota(shape, 1), width.bit_length() - 1) + first_head
    return dot(code, jnp.where(head == want, 1.0, 0.0).astype(BF))


def states_kernel(place, values, log_decay, b_in, mine, other, code, held):
    step = pl.program_id(0)
    tokens, width = values.shape
    heads = log_decay.shape[0]
    n = b_in.shape[1]
    count = width // HDIM
    per_half = mine.shape[1] // width

    @pl.when(step == 0)
    def _():
        code[0:tokens, :] = coded(summed(triangle(tokens, True), log_decay[...]))
        code[tokens:, :] = coded(summed(jnp.ones((TAIL, tokens), BF), log_decay[...]))

    wide = spread(code[...], step * count, heads, HDIM, count)
    scaled = (values[...].astype(F32) * jnp.exp(wide[0:tokens])).astype(BF)
    held[step, 0:n, :] = dot(b_in[...], scaled, 0, 0).astype(BF)
    held[step, n:, :] = tail_of(wide[tokens : tokens + 1])

    @pl.when(step == pl.num_programs(0) - 1)
    def _():
        core = place[3]
        for i in range(per_half):
            mine[:, i * width : (i + 1) * width] = held[core * per_half + i]
            other[:, i * width : (i + 1) * width] = held[(1 - core) * per_half + i]


def chip_kernel(place, mine, theirs, *refs):
    outs, held = refs[:-1], refs[-1]
    n, pw = outs[0].shape[0] - TAIL, outs[0].shape[1]
    core = place[3]
    for g in range(ROW):
        at = slice(g * pw, (g + 1) * pw)
        a, b = mine[0:n, at].astype(F32), theirs[0:n, at].astype(F32)
        ta, tb = tail_total(mine, n, at), tail_total(theirs, n, at)
        state = jnp.where(core == 0, jnp.exp(tb), 1.0) * a + jnp.where(core == 0, 1.0, jnp.exp(ta)) * b
        slot = lax.rem(g - place[0] + ROW, ROW)
        held[slot, 0:n, :] = state.astype(BF)
        held[slot, n:, :] = tail_of(ta + tb)
    for k, out in enumerate(outs):
        out[...] = held[k]


def tail_total(piece, n, lanes):
    tail = piece[n : n + TAIL, lanes].astype(F32)
    return tail[0:1] + tail[1:2] + tail[2:3]


def tail_of(total):
    hi, mid, lo = thirds(total)
    row = iota((TAIL, total.shape[1]), 0)
    tail = jnp.where(row == 0, hi.astype(F32), jnp.where(row == 1, mid.astype(F32), lo.astype(F32)))
    return tail.astype(BF)


def total_of(piece, n):
    tail = piece[n : n + TAIL, :].astype(F32)
    return tail[0:1] + tail[1:2] + tail[2:3]


def row_kernel(place, *refs):
    pieces, out = refs[:-1], refs[-1]
    n = out.shape[0] - TAIL
    me = place[0]
    where = [lax.rem(me - k + ROW, ROW) for k in range(ROW)]
    totals = [total_of(p, n) for p in pieces]
    acc = jnp.zeros((n, out.shape[1]), F32)
    for k in range(ROW):
        later = jnp.zeros_like(totals[0])
        for j in range(ROW):
            if j != k:
                later = later + jnp.where(where[j] > where[k], totals[j], 0.0)
        acc = acc + jnp.exp(later) * pieces[k][0:n, :].astype(F32)
    total = totals[0]
    for j in range(1, ROW):
        total = total + totals[j]
    out[0:n, :] = acc.astype(BF)
    out[n:, :] = tail_of(total)


def enter_kernel(place, *refs):
    pieces, rows = refs[:ROW], refs[ROW : ROW + 3]
    outs, held, totals, sent = refs[ROW + 3 : 2 * ROW + 3], refs[-3], refs[-2], refs[-1]
    n = outs[0].shape[0]
    me = place[0]
    for k in range(ROW):
        slot = lax.rem(me - k + ROW, ROW)
        held[slot] = pieces[k][0:n, :]
        totals[slot] = jnp.broadcast_to(total_of(pieces[k], n), totals.shape[1:])
    one, two, three = rows
    level = place[1]
    near = total_of(one, n)
    zero = jnp.zeros_like(near)
    enter = jnp.where(level > 0, zero + 1.0, zero) * one[0:n, :].astype(F32)
    enter = enter + jnp.where(level > 1, jnp.exp(near), zero) * two[0:n, :].astype(F32)
    near = near + total_of(two, n)
    enter = enter + jnp.where(level > 2, jnp.exp(near), zero) * three[0:n, :].astype(F32)
    for q in range(ROW):
        sent[lax.rem(q - me + ROW, ROW)] = enter.astype(BF)
        if q + 1 < ROW:
            enter = jnp.exp(totals[q][0:1]) * enter + held[q].astype(F32)
    for k in range(ROW):
        outs[k][...] = sent[k]


def local_part(skip, first_head, vals, code, log_decay, b_in, c_in, emit):
    tokens, width = vals.shape
    hdim = width // GH
    blocks = tokens // Q
    columns = spread(code, first_head, code.shape[1] // 3, Q, GH)
    parts = jnp.concatenate([p.astype(F32) for p in thirds(log_decay)], axis=0).astype(BF)
    line = dot(parts, triangle(tokens), 1, 1)
    line = line[0:GH] + line[GH : 2 * GH] + line[2 * GH : 3 * GH]
    scores = dot(c_in, b_in, 1, 1)
    keep = iota((Q, Q), 0) >= iota((Q, Q), 1)
    lanes = iota((Q, 2 * hdim), 1) < hdim
    for pair in range(GH // 2):
        col = slice(pair * 2 * hdim, (pair + 1) * 2 * hdim)
        mine = vals[:, col]
        halves = [
            [jnp.where(lanes, mine[j * Q : (j + 1) * Q], 0).astype(BF) for j in range(blocks)],
            [jnp.where(lanes, 0, mine[j * Q : (j + 1) * Q]).astype(BF) for j in range(blocks)],
        ]
        gain = jnp.where(lanes[0:1], skip[first_head + 2 * pair], skip[first_head + 2 * pair + 1])
        for i in range(blocks):
            left, right = [], []
            for side in range(2):
                head = 2 * pair + side
                for j in range(i + 1):
                    gap = columns[i * Q : (i + 1) * Q, head * Q : (head + 1) * Q]
                    gap = gap - line[head : head + 1, j * Q : (j + 1) * Q]
                    if i == j:
                        gap = jnp.where(keep, gap, -1e30)
                    here = scores[i * Q : (i + 1) * Q, j * Q : (j + 1) * Q]
                    left.append((here * jnp.exp(gap)).astype(BF))
                    right.append(halves[side][j])
            acc = dot(jnp.concatenate(left, axis=1), jnp.concatenate(right, axis=0))
            emit(i, pair * 2 * hdim, acc + gain * mine[i * Q : (i + 1) * Q].astype(F32))


def first_local_kernel(skip, values, all_decay, log_decay, b_in, c_in, out, code):
    step = pl.program_id(0)
    tokens, width = values.shape
    heads = all_decay.shape[0]
    ends = out.shape[1] - 2 * Q

    @pl.when(step == 0)
    def _():
        sums = summed(triangle(tokens), all_decay[...])
        code[...] = coded(sums)
        out[:, ends : ends + Q] = c_in[...]
        decay = jnp.concatenate([jnp.exp(sums), jnp.zeros((tokens, Q - heads), F32)], axis=1)
        out[:, ends + Q :] = decay.astype(BF)

    def emit(i, lane, x):
        at = pl.multiple_of(step * width + lane, Q)
        out[i * Q : (i + 1) * Q, pl.ds(at, x.shape[1])] = x.astype(BF)

    local_part(skip, step * GH, values[...], code[...], log_decay[...], b_in[...], c_in[...], emit)


def local_kernel(first_group, skip, values, log_decay, code, b_in, c_in, out):
    group = pl.program_id(0) + first_group

    def emit(i, lane, x):
        out[i * Q : (i + 1) * Q, lane : lane + x.shape[1]] = x.astype(out.dtype)

    local_part(skip, group * GH, values[...], code[...], log_decay[...], b_in[...], c_in[...], emit)


def split_kernel(place, mine, theirs, *refs):
    enters, keep, give, held = refs[:ROW], refs[ROW], refs[ROW + 1], refs[ROW + 2]
    n, pw = enters[0].shape
    core = place[3]
    for k in range(ROW):
        held[lax.rem(place[0] - k + ROW, ROW)] = enters[k][...]

    def emit(earlier, first, second):
        for g in range(ROW):
            at = slice(g * pw, (g + 1) * pw)
            enter = held[g]
            decay = jnp.exp(tail_total(earlier, n, at))
            first[:, at] = enter
            second[:, at] = (decay * enter.astype(F32) + earlier[0:n, at].astype(F32)).astype(BF)

    @pl.when(core == 0)
    def _():
        emit(mine, keep, give)

    @pl.when(core != 0)
    def _():
        emit(theirs, give, keep)


def sorted_kernel(place, keep, got, early, late):
    half = keep.shape[1]
    cut = early.shape[1]

    def emit(first, second):
        lo = min(cut, half)
        early[:, 0:lo] = first[:, 0:lo]
        if cut < half:
            late[:, 0 : half - cut] = first[:, cut:]
            late[:, half - cut :] = second[...]
        else:
            early[:, half:] = second[:, 0 : cut - half]
            late[...] = second[:, cut - half :]

    @pl.when(place[3] == 0)
    def _():
        emit(keep, got)

    @pl.when(place[3] != 0)
    def _():
        emit(got, keep)


def owned_plan(place, owner, docs):
    me = place[2]
    plans = []
    for r in range(docs):
        doc = lax.rem(me + r, docs)
        first, second = owner[doc, 0] == me, owner[doc, 1] == me
        plans.append((doc, first, second))
    return plans


def write_owned(plan, r, rows, out, lanes, sems, zeros=None, act="start"):
    doc, first, second = plan
    both = jnp.logical_and(first, second)

    def go(when, source, to, i):
        @pl.when(when)
        def _():
            copy = pltpu.make_async_copy(source, out.at[to, :, lanes], sems.at[2 * r + i])
            copy.start() if act == "start" else copy.wait()

    if rows is not None:
        go(first, rows.at[0:Q], 2 * doc, 0)
        go(jnp.logical_and(jnp.logical_not(first), second), rows.at[Q : 2 * Q], 2 * doc, 0)
        go(both, rows.at[Q : 2 * Q], 2 * doc + 1, 1)
    if zeros is not None:
        go(jnp.logical_not(jnp.logical_or(first, second)), zeros, 2 * doc, 0)
        go(jnp.logical_not(both), zeros, 2 * doc + 1, 1)


def read_part(sources, r, target, sems, act="start"):
    copy = pltpu.make_async_copy(sources[r], target.at[r], sems.at[r])
    copy.start() if act == "start" else copy.wait()


def finish_kernel(place, owner, *refs):
    firsts, others, enters = refs[0:4], refs[4:8], refs[8:12]
    out, first, other, enter, done, zeros, s_first, s_other, s_enter, s_out, s_zero = refs[12:]
    plans = owned_plan(place, owner, 4)
    groups = ((firsts, first, s_first), (others, other, s_other), (enters, enter, s_enter))
    lanes = pl.ds(0, done.shape[2])

    def some(plan):
        return jnp.logical_or(plan[1], plan[2])

    for r, plan in enumerate(plans):

        @pl.when(some(plan))
        def _():
            for sources, target, sems in groups:
                read_part(sources, r, target, sems)

    zeros[...] = jnp.zeros_like(zeros)
    for r, plan in enumerate(plans):
        write_owned(plan, r, None, out, pl.ds(0, zeros.shape[1]), s_zero, zeros)

    ends = first.shape[2] - 2 * Q
    step = 512
    for r, plan in enumerate(plans):

        @pl.when(some(plan))
        def _():
            for sources, target, sems in groups:
                read_part(sources, r, target, sems, "wait")
            c = first[r, :, ends : ends + Q]
            decay = first[r, :, ends + Q :]
            for at in range(0, done.shape[2], step):
                head = iota((Q, step), 0)
                pick = jnp.where(head == (iota((Q, step), 1) + at) // HDIM, 1.0, 0.0).astype(BF)
                add = dot(decay, pick) * dot(c, enter[r, :, at : at + step])
                here = first[r, :, at : at + step] if at < ends else other[r, :, at - ends : at - ends + step]
                done[r, :, at : at + step] = (here.astype(F32) + add).astype(BF)

        write_owned(plan, r, done.at[r], out, lanes, s_out)
    for r, plan in enumerate(plans):
        write_owned(plan, r, done.at[r], out, lanes, s_out, None, "wait")
        write_owned(plan, r, None, out, pl.ds(0, zeros.shape[1]), s_zero, zeros, "wait")


def owned_kernel(first_lane, place, owner, *refs):
    sources = refs[:4]
    out, held, s_in, s_out = refs[-4:]
    plans = owned_plan(place, owner, 4)
    lanes = pl.ds(first_lane, held.shape[2])
    for act in ("start", "wait"):
        for r, plan in enumerate(plans):

            @pl.when(jnp.logical_or(plan[1], plan[2]))
            def _():
                read_part(sources, r, held, s_in, act)

            if act == "wait":
                write_owned(plan, r, held.at[r], out, lanes, s_out)
    for r, plan in enumerate(plans):
        write_owned(plan, r, held.at[r], out, lanes, s_out, None, "wait")


def carried_kernel(first_head, enter, local, code, c_in, out):
    step = pl.program_id(0)
    width = local.shape[1]
    count = width // HDIM
    decay = jnp.exp(spread(code[...], first_head + step * count, code.shape[1] // 3, HDIM, count))
    out[...] = (local[...] + decay * dot(c_in[...], enter[...])).astype(BF)


def near(arrays):
    return [pltpu.with_memory_space_constraint(x, pltpu.VMEM) for x in arrays]


def whole_spec(shape):
    return pl.BlockSpec(shape, lambda *_: (0,) * len(shape))


def whole(values, b_in, c_in, log_decay, skip, owner):
    seq_n = lax.axis_size("seq")
    doc_n = lax.axis_size("doc")
    per_level = ROW * CORES
    levels = seq_n // per_level
    values, b_in, c_in, log_decay = values[0], b_in[0], c_in[0], log_decay[0]
    tokens, width = values.shape
    heads = log_decay.shape[0]
    n = b_in.shape[1]
    groups = heads // GH
    gw = width // groups
    seq_at = lax.axis_index("seq")
    doc_at = lax.axis_index("doc")
    place = jnp.stack([seq_at % per_level // CORES, seq_at // per_level, doc_at, seq_at % CORES]).astype(jnp.int32)

    def shifted(x, step_x=0, step_z=0, swap=0):
        pairs = []
        for i in range(seq_n):
            z, at, core = i // per_level, i % per_level // CORES, i % CORES
            z, at, core = (z + step_z) % levels, (at + step_x) % ROW, (core + swap) % CORES
            pairs.append((i, z * per_level + at * CORES + core))
        return lax.ppermute(x, "seq", pairs)

    def along_row(pieces):
        return [pieces[0]] + [shifted(pieces[k], step_x=k) for k in range(1, ROW)]

    def over_docs(x, k):
        return lax.ppermute(x, "doc", [(d, (d + k) % doc_n) for d in range(doc_n)])

    def over_all_docs(x, far_by):
        before = over_docs(x, 1)
        after = over_docs(x, doc_n - 1)
        far = over_docs(before, 1) if far_by > 0 else over_docs(after, doc_n - 1)
        return [x, after, far, before]

    smem = pl.BlockSpec(memory_space=pltpu.SMEM)
    vmem = pl.BlockSpec(memory_space=pltpu.VMEM)
    anywhere = pl.BlockSpec(memory_space=pl.ANY)
    prefetch = pltpu.PrefetchScalarGridSpec
    code_shape = jax.ShapeDtypeStruct((tokens, 3 * heads), BF)
    early = sum(EARLY)
    early_width = early * HDIM

    first_width = EARLY[0] * HDIM
    first, code = pl.pallas_call(
        first_local_kernel,
        name="local_first",
        out_shape=[jax.ShapeDtypeStruct((tokens, first_width + 2 * Q), BF), code_shape],
        grid=(EARLY[0] // GH,),
        in_specs=[
            smem,
            pl.BlockSpec((tokens, gw), lambda g: (0, g)),
            whole_spec((heads, tokens)),
            pl.BlockSpec((GH, tokens), lambda g: (g, 0)),
            whole_spec((tokens, n)),
            whole_spec((tokens, n)),
        ],
        out_specs=[whole_spec((tokens, first_width + 2 * Q)), whole_spec(code_shape.shape)],
    )(skip, values, log_decay, log_decay, b_in, c_in)
    firsts = over_all_docs(first, 1)

    half = width // CORES
    pw = half // ROW
    half_shape = jax.ShapeDtypeStruct((n + TAIL, half), BF)
    piece = jax.ShapeDtypeStruct((n + TAIL, pw), BF)
    mine, other_half = pl.pallas_call(
        states_kernel,
        name="states",
        out_shape=[half_shape] * 2,
        grid_spec=prefetch(
            num_scalar_prefetch=1,
            grid=(width // WIDE,),
            in_specs=[
                pl.BlockSpec((tokens, WIDE), lambda k, at: (0, k)),
                whole_spec((heads, tokens)),
                whole_spec((tokens, n)),
            ],
            out_specs=[whole_spec(half_shape.shape)] * 2,
            scratch_shapes=[
                pltpu.VMEM((tokens + TAIL, 3 * heads), BF),
                pltpu.VMEM((width // WIDE, n + TAIL, WIDE), BF),
            ],
        ),
    )(place, values, log_decay, b_in)
    theirs = shifted(other_half, swap=1)
    pieces = pl.pallas_call(
        chip_kernel,
        name="chip",
        out_shape=[piece] * ROW,
        in_specs=[smem, vmem, vmem],
        out_specs=[vmem] * ROW,
        scratch_shapes=[pltpu.VMEM((ROW,) + piece.shape, BF)],
    )(place, *near([mine, theirs]))
    pieces = along_row(pieces)

    def local_of(start, count, dtype):
        base = start // GH
        return pl.pallas_call(
            functools.partial(local_kernel, base),
            out_shape=jax.ShapeDtypeStruct((tokens, count * HDIM), dtype),
            grid=(count // GH,),
            in_specs=[
                smem,
                pl.BlockSpec((tokens, gw), lambda g: (0, g + base)),
                pl.BlockSpec((GH, tokens), lambda g: (g + base, 0)),
                whole_spec(code.shape),
                whole_spec((tokens, n)),
                whole_spec((tokens, n)),
            ],
            out_specs=pl.BlockSpec((tokens, gw), lambda g: (0, g)),
        )(skip, values, log_decay, code, b_in, c_in)

    other = local_of(EARLY[0], EARLY[1], BF)
    others = over_all_docs(other, -1)
    late_local = local_of(early, heads - early, F32)

    row = pl.pallas_call(
        row_kernel, name="row", out_shape=piece, in_specs=[smem] + [vmem] * ROW, out_specs=vmem
    )(place, *near(pieces))
    rows = [shifted(row, step_z=k) for k in (1, 2, 3)]
    enter = jax.ShapeDtypeStruct((n, pw), BF)
    enters = pl.pallas_call(
        enter_kernel,
        name="enter",
        out_shape=[enter] * ROW,
        in_specs=[smem] + [vmem] * (ROW + 3),
        out_specs=[vmem] * ROW,
        scratch_shapes=[
            pltpu.VMEM((ROW, n, pw), BF),
            pltpu.VMEM((ROW, 8, pw), F32),
            pltpu.VMEM((ROW, n, pw), BF),
        ],
    )(place, *near(pieces + rows))
    enters = along_row(enters)
    keep, give = pl.pallas_call(
        split_kernel,
        name="split",
        out_shape=[jax.ShapeDtypeStruct((n, half), BF)] * 2,
        in_specs=[smem] + [vmem] * (ROW + 2),
        out_specs=[vmem] * 2,
        scratch_shapes=[pltpu.VMEM((ROW, n, pw), BF)],
    )(place, *near([mine, theirs] + enters))
    got = shifted(give, swap=1)
    enter_early, enter_late = pl.pallas_call(
        sorted_kernel,
        name="sorted",
        out_shape=[
            jax.ShapeDtypeStruct((n, early_width), BF),
            jax.ShapeDtypeStruct((n, width - early_width), BF),
        ],
        in_specs=[smem] + [vmem] * 2,
        out_specs=[vmem] * 2,
    )(place, *near([keep, got]))
    early_enters = over_all_docs(enter_early, 1)

    late_width = width - early_width
    late = pl.pallas_call(
        functools.partial(carried_kernel, early),
        name="carried",
        out_shape=jax.ShapeDtypeStruct((tokens, late_width), BF),
        grid=(late_width // gw,),
        in_specs=[
            pl.BlockSpec((n, gw), lambda k: (0, k)),
            pl.BlockSpec((tokens, gw), lambda k: (0, k)),
            whole_spec(code.shape),
            whole_spec((tokens, n)),
        ],
        out_specs=pl.BlockSpec((tokens, gw), lambda k: (0, k)),
    )(enter_late, late_local, code, c_in)
    lates = over_all_docs(late, -1)

    dma = pltpu.SemaphoreType.DMA
    result = jax.ShapeDtypeStruct((doc_n * 2, Q, width), BF)
    owned = pl.pallas_call(
        finish_kernel,
        name="finish",
        out_shape=result,
        in_specs=[smem] * 2 + [anywhere] * 12,
        out_specs=anywhere,
        scratch_shapes=[
            pltpu.VMEM((doc_n,) + first.shape, BF),
            pltpu.VMEM((doc_n,) + other.shape, BF),
            pltpu.VMEM((doc_n,) + enter_early.shape, BF),
            pltpu.VMEM((doc_n, tokens, early_width), BF),
            pltpu.VMEM((Q, width), BF),
            dma((doc_n,)),
            dma((doc_n,)),
            dma((doc_n,)),
            dma((doc_n * 2,)),
            dma((doc_n * 2,)),
        ],
    )(place, owner, *firsts, *others, *early_enters)
    owned = pl.pallas_call(
        functools.partial(owned_kernel, early_width),
        name="owned",
        out_shape=result,
        in_specs=[smem] * 2 + [anywhere] * 5,
        out_specs=anywhere,
        scratch_shapes=[pltpu.VMEM((doc_n,) + late.shape, BF), dma((doc_n,)), dma((doc_n * 2,))],
        input_output_aliases={6: 0},
    )(place, owner, *lates, owned)
    return owned[None]


def solution(mesh):
    in_specs = (
        P("doc", "seq", None),
        P("doc", "seq", None),
        P("doc", "seq", None),
        P("doc", None, "seq"),
        P(),
        P(None, "seq"),
    )
    out_specs = P("doc", "seq", None, None)
    return jax.shard_map(whole, mesh=mesh, in_specs=in_specs, out_specs=out_specs, check_vma=False)
```

```python
import functools

import jax
import jax.numpy as jnp
from jax import lax
from jax.experimental import pallas as pl
from jax.experimental.pallas import tpu as pltpu
from jax.sharding import PartitionSpec as P

Q = 128
ROW = 4
CORES = 2
GH = 8
HDIM = 64
WIDE = 1024
EARLY = (24, 16)
TAIL = 16
LOG2E = 1.4426950408889634
F32 = jnp.float32
BF = jnp.bfloat16


def iota(shape, dim):
    return lax.broadcasted_iota(jnp.int32, shape, dim)


def dot(a, b, ca=1, cb=0):
    return lax.dot_general(a, b, (((ca,), (cb,)), ((), ())), preferred_element_type=F32)


def core_at():
    return lax.rem(lax.axis_index("seq"), CORES)


def row_at():
    return lax.rem(lax.div(lax.axis_index("seq"), CORES), ROW)


def level_at():
    return lax.div(lax.axis_index("seq"), CORES * ROW)


def thirds(x):
    hi = x.astype(BF)
    rest = x - hi.astype(F32)
    mid = rest.astype(BF)
    lo = (rest - mid.astype(F32)).astype(BF)
    return hi, mid, lo


def triangle(n, strict_upper=False):
    rows, cols = iota((n, n), 0), iota((n, n), 1)
    keep = cols > rows if strict_upper else cols <= rows
    return jnp.where(keep, 1.0, 0.0).astype(BF)


def summed(weights, log_decay):
    heads = log_decay.shape[0]
    parts = jnp.concatenate([p.astype(F32) for p in thirds(log_decay)], axis=0).astype(BF)
    sums = dot(weights, parts, 1, 1)
    return sums[:, 0:heads] + sums[:, heads : 2 * heads] + sums[:, 2 * heads : 3 * heads]


def states_kernel(values_at, decay_at, b_at, mine, other, values, log_decay, b_in, pick, held, sems):
    tokens, width = values.shape
    wait = bring(((decay_at, log_decay), (b_at, b_in)), values_at, 0, values, WIDE, sems)
    n = b_in.shape[1]
    count = WIDE // HDIM
    steps = width // WIDE
    core = core_at()
    shape = pick.shape
    head = jnp.bitwise_and(iota(shape, 0), count - 1)
    keep = (head == lax.shift_right_logical(iota(shape, 1), HDIM.bit_length() - 1)) & (iota(shape, 0) < 3 * count)
    pick[...] = jnp.where(keep, 1.0, 0.0).astype(BF)
    wait()
    weights = jnp.concatenate([triangle(tokens, True), jnp.ones((TAIL, tokens), BF)], axis=0)
    parts = [p.astype(F32) for p in thirds(summed(weights, log_decay[...] * LOG2E))]
    for i in range(steps):
        cut = [p[:, i * count : (i + 1) * count] for p in parts]
        code = jnp.concatenate(cut + [jnp.zeros_like(cut[0])], axis=1).astype(BF)
        wide = dot(code, pick[...])
        wait(i)
        vals = values[:, i * WIDE : (i + 1) * WIDE].astype(F32)
        scaled = (vals * jnp.exp2(wide[0:tokens])).astype(BF)
        half, at = i * WIDE // mine.shape[1], i * WIDE % mine.shape[1]
        held[half, 0:n, at : at + WIDE] = dot(b_in[...], scaled, 0, 0).astype(BF)
        held[half, n:, at : at + WIDE] = tail_of(wide[tokens : tokens + 1])
    mine[...] = held[core]
    other[...] = held[1 - core]


def chip_kernel(mine, theirs, *refs):
    outs, earlier, held = refs[:-2], refs[-2], refs[-1]
    n, pw = outs[0].shape[0] - TAIL, outs[0].shape[1]
    core = core_at()
    for g in range(ROW):
        at = slice(g * pw, (g + 1) * pw)
        a, b = mine[0:n, at].astype(F32), theirs[0:n, at].astype(F32)
        ta, tb = tail_total(mine, n, at), tail_total(theirs, n, at)
        state = jnp.where(core == 0, jnp.exp2(tb), 1.0) * a + jnp.where(core == 0, 1.0, jnp.exp2(ta)) * b
        slot = lax.rem(g - row_at() + ROW, ROW)
        held[slot, 0:n, :] = state.astype(BF)
        held[slot, n:, :] = tail_of(ta + tb)
    for k, out in enumerate(outs):
        out[...] = held[k]

    @pl.when(core == 0)
    def _():
        earlier[...] = mine[...]

    @pl.when(core != 0)
    def _():
        earlier[...] = theirs[...]


def tail_total(piece, n, lanes):
    tail = piece[n : n + TAIL, lanes].astype(F32)
    return tail[0:1] + tail[1:2] + tail[2:3]


def tail_of(total):
    hi, mid, lo = thirds(total)
    row = iota((TAIL, total.shape[1]), 0)
    tail = jnp.where(row == 0, hi.astype(F32), jnp.where(row == 1, mid.astype(F32), lo.astype(F32)))
    return tail.astype(BF)


def total_of(piece, n):
    tail = piece[n : n + TAIL, :].astype(F32)
    return tail[0:1] + tail[1:2] + tail[2:3]


def row_kernel(*refs):
    pieces, out = refs[:-1], refs[-1]
    n = out.shape[0] - TAIL
    me = row_at()
    where = [lax.rem(me - k + ROW, ROW) for k in range(ROW)]
    totals = [total_of(p, n) for p in pieces]
    acc = jnp.zeros((n, out.shape[1]), F32)
    for k in range(ROW):
        later = jnp.zeros_like(totals[0])
        for j in range(ROW):
            if j != k:
                later = later + jnp.where(where[j] > where[k], totals[j], 0.0)
        acc = acc + jnp.exp2(later) * pieces[k][0:n, :].astype(F32)
    total = totals[0]
    for j in range(1, ROW):
        total = total + totals[j]
    out[0:n, :] = acc.astype(BF)
    out[n:, :] = tail_of(total)


def enter_kernel(*refs):
    pieces, rows = refs[:ROW], refs[ROW : ROW + 3]
    outs, held, totals, sent = refs[ROW + 3 : 2 * ROW + 3], refs[-3], refs[-2], refs[-1]
    n = outs[0].shape[0]
    me = row_at()
    for k in range(ROW):
        slot = lax.rem(me - k + ROW, ROW)
        held[slot] = pieces[k][0:n, :]
        totals[slot] = jnp.broadcast_to(total_of(pieces[k], n), totals.shape[1:])
    one, two, three = rows
    level = level_at()
    near = total_of(one, n)
    zero = jnp.zeros_like(near)
    enter = jnp.where(level > 0, zero + 1.0, zero) * one[0:n, :].astype(F32)
    enter = enter + jnp.where(level > 1, jnp.exp2(near), zero) * two[0:n, :].astype(F32)
    near = near + total_of(two, n)
    enter = enter + jnp.where(level > 2, jnp.exp2(near), zero) * three[0:n, :].astype(F32)
    for q in range(ROW):
        sent[lax.rem(q - me + ROW, ROW)] = enter.astype(BF)
        if q + 1 < ROW:
            enter = jnp.exp2(totals[q][0:1]) * enter + held[q].astype(F32)
    for k in range(ROW):
        outs[k][...] = sent[k]


def token_sums(lower, log_decay):
    heads = log_decay.shape[0]
    parts = jnp.concatenate([p.astype(F32) for p in thirds(log_decay * LOG2E)], axis=0).astype(BF)
    sums = dot(lower, parts, 1, 1)
    line = dot(parts, lower, 1, 1)
    return (
        sums[:, 0:heads] + sums[:, heads : 2 * heads] + sums[:, 2 * heads : 3 * heads],
        line[0:heads] + line[heads : 2 * heads] + line[2 * heads : 3 * heads],
    )


def local_part(skip, first_head, vals, sums, line, scores, emit):
    tokens, width = vals.shape
    hdim = width // GH
    blocks = tokens // Q
    keep = iota((Q, Q), 0) >= iota((Q, Q), 1)
    lanes = iota((Q, 2 * hdim), 1) < hdim
    for pair in range(GH // 2):
        col = slice(pair * 2 * hdim, (pair + 1) * 2 * hdim)
        mine = vals[:, col]
        halves = [
            [jnp.where(lanes, mine[j * Q : (j + 1) * Q], 0).astype(BF) for j in range(blocks)],
            [jnp.where(lanes, 0, mine[j * Q : (j + 1) * Q]).astype(BF) for j in range(blocks)],
        ]
        gain = jnp.where(lanes[0:1], skip[first_head + 2 * pair], skip[first_head + 2 * pair + 1])
        for i in range(blocks):
            left, right = [], []
            for side in range(2):
                head = 2 * pair + side
                column = jnp.broadcast_to(sums[i * Q : (i + 1) * Q, head : head + 1], (Q, Q))
                for j in range(i + 1):
                    gap = column - line[head : head + 1, j * Q : (j + 1) * Q]
                    if i == j:
                        gap = jnp.where(keep, gap, -1e30)
                    here = scores[i * Q : (i + 1) * Q, j * Q : (j + 1) * Q]
                    left.append((here * jnp.exp2(gap)).astype(BF))
                    right.append(halves[side][j])
            acc = dot(jnp.concatenate(left, axis=1), jnp.concatenate(right, axis=0))
            emit(i, pair * 2 * hdim, acc + gain * mine[i * Q : (i + 1) * Q].astype(F32))


def bring(small, values_at, first_lane, values, width, sems):
    n = len(small)
    copies = [pltpu.make_async_copy(x, y, sems.at[i]) for i, (x, y) in enumerate(small)]

    def lanes(i):
        at = i * width
        if not isinstance(i, int):
            at = pl.multiple_of(at, width)
        return pltpu.make_async_copy(
            values_at.at[:, pl.ds(first_lane + at, width)], values.at[:, pl.ds(at, width)], sems.at[n + i]
        )

    for copy in copies:
        copy.start()
    for i in range(values.shape[1] // width):
        lanes(i).start()

    def wait(i=None):
        if i is not None:
            lanes(i).wait()
            return
        for copy in copies:
            copy.wait()

    return wait


def local_groups(start, skip, values, sums, line, scores, emit, wait):
    width = GH * HDIM
    for i in range(values.shape[1] // width):
        wait(i)
        heads = slice(i * GH, (i + 1) * GH)

        def put(block, lane, x):
            emit(block, i * width + lane, x)

        vals = values[:, i * width : (i + 1) * width]
        local_part(skip, start + i * GH, vals, sums[:, heads], line[heads], scores, put)


def first_local_kernel(skip, values_at, decay_at, b_at, c_at, out, values, log_decay, b_in, c_in, lower, scores, sems):
    tokens = values.shape[0]
    heads = log_decay.shape[0]
    ends = out.shape[1] - 2 * Q
    small = ((decay_at, log_decay), (b_at, b_in), (c_at, c_in))
    wait = bring(small, values_at, 0, values, GH * HDIM, sems)
    lower[...] = triangle(tokens)
    wait()
    scores[...] = dot(c_in[...], b_in[...], 1, 1)
    sums, line = token_sums(lower[...], log_decay[...])
    out[:, ends : ends + Q] = c_in[...]
    decay = jnp.concatenate([jnp.exp2(sums), jnp.zeros((tokens, Q - heads), F32)], axis=1)
    out[:, ends + Q :] = decay.astype(BF)

    def emit(i, at, x):
        out[i * Q : (i + 1) * Q, at : at + x.shape[1]] = x.astype(BF)

    local_groups(0, skip, values, sums, line, scores, emit, wait)


def other_local_kernel(start, skip, values_at, decay_at, b_at, c_at, out, values, log_decay, b_in, c_in, lower, scores, sems):
    small = ((decay_at, log_decay), (b_at, b_in), (c_at, c_in))
    wait = bring(small, values_at, start * HDIM, values, GH * HDIM, sems)
    lower[...] = triangle(values.shape[0])
    wait()
    scores[...] = dot(c_in[...], b_in[...], 1, 1)
    count = values.shape[1] // HDIM
    sums, line = token_sums(lower[...], log_decay[start : start + count, :])

    def emit(i, at, x):
        out[i * Q : (i + 1) * Q, at : at + x.shape[1]] = x.astype(BF)

    local_groups(start, skip, values, sums, line, scores, emit, wait)


def late_kernel(
    start, skip, enter, first_at, values_at, decay_at, b_at, c_at, out,
    decays, values, log_decay, b_in, c_in, lower, scores, sems,
):
    small = (
        (decay_at, log_decay),
        (b_at, b_in),
        (c_at, c_in),
        (first_at.at[:, pl.ds(first_at.shape[1] - Q, Q)], decays),
    )
    wait = bring(small, values_at, start * HDIM, values, GH * HDIM, sems)
    lower[...] = triangle(values.shape[0])
    wait()
    scores[...] = dot(c_in[...], b_in[...], 1, 1)
    count = values.shape[1] // HDIM
    sums, line = token_sums(lower[...], log_decay[start : start + count, :])
    row = iota((Q, Q), 0)
    side = lax.shift_right_logical(iota((Q, Q), 1), HDIM.bit_length() - 1)

    def emit(i, at, x):
        pick = jnp.where(row == side + (start + at // HDIM), 1.0, 0.0).astype(BF)
        rows = slice(i * Q, (i + 1) * Q)
        add = dot(decays[rows, :], pick) * dot(c_in[rows, :], enter[:, at : at + Q])
        out[rows, at : at + Q] = (x + add).astype(BF)

    local_groups(start, skip, values, sums, line, scores, emit, wait)


def put_half(half, lanes, value, early, late):
    at = half * (early.shape[1] + late.shape[1]) // CORES + lanes.start
    size = lanes.stop - lanes.start
    if at + size <= early.shape[1]:
        early[:, at : at + size] = value
    else:
        late[:, at - early.shape[1] : at - early.shape[1] + size] = value


def split_kernel(earlier, *refs):
    enters, early, late, give, held = refs[:ROW], refs[ROW], refs[ROW + 1], refs[ROW + 2], refs[ROW + 3]
    n, pw = enters[0].shape
    core = core_at()
    for k in range(ROW):
        held[lax.rem(row_at() - k + ROW, ROW)] = enters[k][...]

    def emit(half):
        for g in range(ROW):
            at = slice(g * pw, (g + 1) * pw)
            enter = held[g]
            decay = jnp.exp2(tail_total(earlier, n, at))
            after = (decay * enter.astype(F32) + earlier[0:n, at].astype(F32)).astype(BF)
            put_half(half, at, enter if half == 0 else after, early, late)
            give[:, at] = after if half == 0 else enter

    for half in range(CORES):

        @pl.when(core == half)
        def _():
            emit(half)


def sorted_kernel(got, early_in, late_in, early, late):
    for half in range(CORES):

        @pl.when(core_at() != half)
        def _():
            for at in range(0, got.shape[1], GH * HDIM):
                lanes = slice(at, at + GH * HDIM)
                put_half(half, lanes, got[:, lanes], early, late)


def owned_plan(owner, docs):
    me = lax.axis_index("doc")
    plans = []
    for r in range(docs):
        doc = lax.rem(me + r, docs)
        first, second = owner[doc, 0] == me, owner[doc, 1] == me
        plans.append((doc, first, second))
    return plans


def write_owned(plan, r, rows, out, lanes, sems, zeros=None, act="start"):
    doc, first, second = plan
    both = jnp.logical_and(first, second)

    def go(when, source, to, i):
        @pl.when(when)
        def _():
            copy = pltpu.make_async_copy(source, out.at[to, :, lanes], sems.at[2 * r + i])
            copy.start() if act == "start" else copy.wait()

    if rows is not None:
        go(first, rows.at[0:Q], 2 * doc, 0)
        go(jnp.logical_and(jnp.logical_not(first), second), rows.at[Q : 2 * Q], 2 * doc, 0)
        go(both, rows.at[Q : 2 * Q], 2 * doc + 1, 1)
    if zeros is not None:
        go(jnp.logical_not(jnp.logical_or(first, second)), zeros, 2 * doc, 0)
        go(jnp.logical_not(both), zeros, 2 * doc + 1, 1)


def read_part(sources, r, target, sems, act="start"):
    copy = pltpu.make_async_copy(sources[r], target.at[r], sems.at[r])
    copy.start() if act == "start" else copy.wait()


def finish_kernel(owner, *refs):
    firsts, others, enters = refs[0:4], refs[4:8], refs[8:12]
    out, first, other, enter, done, zeros, s_first, s_other, s_enter, s_out, s_zero = refs[12:]
    plans = owned_plan(owner, 4)
    groups = ((firsts, first, s_first), (others, other, s_other), (enters, enter, s_enter))
    lanes = pl.ds(0, done.shape[2])

    def some(plan):
        return jnp.logical_or(plan[1], plan[2])

    for r, plan in enumerate(plans):

        @pl.when(some(plan))
        def _():
            for sources, target, sems in groups:
                read_part(sources, r, target, sems)

    zeros[...] = jnp.zeros_like(zeros)
    for r, plan in enumerate(plans):
        write_owned(plan, r, None, out, pl.ds(0, zeros.shape[1]), s_zero, zeros)

    ends = first.shape[2] - 2 * Q
    step = 512
    for r, plan in enumerate(plans):

        @pl.when(some(plan))
        def _():
            for sources, target, sems in groups:
                read_part(sources, r, target, sems, "wait")
            c = first[r, :, ends : ends + Q]
            decay = first[r, :, ends + Q :]
            for at in range(0, done.shape[2], step):
                head = iota((Q, step), 0)
                pick = jnp.where(head == (iota((Q, step), 1) + at) // HDIM, 1.0, 0.0).astype(BF)
                add = dot(decay, pick) * dot(c, enter[r, :, at : at + step])
                here = first[r, :, at : at + step] if at < ends else other[r, :, at - ends : at - ends + step]
                done[r, :, at : at + step] = (here.astype(F32) + add).astype(BF)

        write_owned(plan, r, done.at[r], out, lanes, s_out)
    for r, plan in enumerate(plans):
        write_owned(plan, r, done.at[r], out, lanes, s_out, None, "wait")
        write_owned(plan, r, None, out, pl.ds(0, zeros.shape[1]), s_zero, zeros, "wait")


def owned_kernel(first_lane, owner, *refs):
    sources = refs[:4]
    out, held, s_in, s_out = refs[-4:]
    plans = owned_plan(owner, 4)
    lanes = pl.ds(first_lane, held.shape[2])
    for act in ("start", "wait"):
        for r, plan in enumerate(plans):

            @pl.when(jnp.logical_or(plan[1], plan[2]))
            def _():
                read_part(sources, r, held, s_in, act)

            if act == "wait":
                write_owned(plan, r, held.at[r], out, lanes, s_out)
    for r, plan in enumerate(plans):
        write_owned(plan, r, held.at[r], out, lanes, s_out, None, "wait")


def inside(shape):
    return pltpu.VMEM(shape.shape, shape.dtype)


def near(arrays):
    return [pltpu.with_memory_space_constraint(x, pltpu.VMEM) for x in arrays]


def far(arrays):
    return [pltpu.with_memory_space_constraint(x, pltpu.HBM) for x in arrays]


def whole(values, b_in, c_in, log_decay, skip, owner):
    seq_n = lax.axis_size("seq")
    doc_n = lax.axis_size("doc")
    per_level = ROW * CORES
    levels = seq_n // per_level
    values, b_in, c_in, log_decay = values[0], b_in[0], c_in[0], log_decay[0]
    tokens, width = values.shape
    heads = log_decay.shape[0]
    n = b_in.shape[1]

    def shifted(x, step_x=0, step_z=0, swap=0):
        pairs = []
        for i in range(seq_n):
            z, at, core = i // per_level, i % per_level // CORES, i % CORES
            z, at, core = (z + step_z) % levels, (at + step_x) % ROW, (core + swap) % CORES
            pairs.append((i, z * per_level + at * CORES + core))
        return lax.ppermute(x, "seq", pairs)

    def along_row(pieces):
        return [pieces[0]] + [shifted(pieces[k], step_x=k) for k in range(1, ROW)]

    def over_docs(x, k):
        return lax.ppermute(x, "doc", [(d, (d + k) % doc_n) for d in range(doc_n)])

    def over_all_docs(x, far_by):
        before = over_docs(x, 1)
        after = over_docs(x, doc_n - 1)
        far = over_docs(before, 1) if far_by > 0 else over_docs(after, doc_n - 1)
        return [x, after, far, before]

    smem = pl.BlockSpec(memory_space=pltpu.SMEM)
    vmem = pl.BlockSpec(memory_space=pltpu.VMEM)
    anywhere = pl.BlockSpec(memory_space=pl.ANY)
    early = sum(EARLY)
    early_width = early * HDIM

    first_width = EARLY[0] * HDIM
    dma = pltpu.SemaphoreType.DMA

    def local_scratch(count, small=3):
        return [
            pltpu.VMEM((tokens, count * HDIM), BF),
            pltpu.VMEM((heads, tokens), F32),
            pltpu.VMEM((tokens, n), BF),
            pltpu.VMEM((tokens, n), BF),
            pltpu.VMEM((tokens, tokens), BF),
            pltpu.VMEM((tokens, tokens), F32),
            dma((small + count // GH,)),
        ]

    first = pl.pallas_call(
        first_local_kernel,
        name="local_first",
        out_shape=jax.ShapeDtypeStruct((tokens, first_width + 2 * Q), BF),
        in_specs=[smem] + [anywhere] * 4,
        out_specs=vmem,
        scratch_shapes=local_scratch(EARLY[0]),
    )(skip, values, log_decay, b_in, c_in)
    firsts = over_all_docs(first, -1)

    half = width // CORES
    pw = half // ROW
    half_shape = jax.ShapeDtypeStruct((n + TAIL, half), BF)
    piece = jax.ShapeDtypeStruct((n + TAIL, pw), BF)
    mine, other_half = pl.pallas_call(
        states_kernel,
        name="states",
        out_shape=[inside(half_shape)] * 2,
        in_specs=[anywhere] * 3,
        out_specs=[vmem] * 2,
        scratch_shapes=[
            pltpu.VMEM((tokens, width), BF),
            pltpu.VMEM((heads, tokens), F32),
            pltpu.VMEM((tokens, n), BF),
            pltpu.VMEM((4 * WIDE // HDIM, WIDE), BF),
            pltpu.VMEM((CORES,) + half_shape.shape, BF),
            dma((2 + width // WIDE,)),
        ],
    )(values, log_decay, b_in)
    theirs = shifted(other_half, swap=1)
    *pieces, earlier = pl.pallas_call(
        chip_kernel,
        name="chip",
        out_shape=[inside(piece)] * ROW + [inside(half_shape)],
        in_specs=[vmem, vmem],
        out_specs=[vmem] * (ROW + 1),
        scratch_shapes=[pltpu.VMEM((ROW,) + piece.shape, BF)],
    )(*near([mine, theirs]))
    pieces = along_row(pieces)

    other = pl.pallas_call(
        functools.partial(other_local_kernel, EARLY[0]),
        name="local_other",
        out_shape=jax.ShapeDtypeStruct((tokens, EARLY[1] * HDIM), BF),
        in_specs=[smem] + [anywhere] * 4,
        out_specs=vmem,
        scratch_shapes=local_scratch(EARLY[1]),
    )(skip, values, log_decay, b_in, c_in)
    others = over_all_docs(other, 1)

    row = pl.pallas_call(
        row_kernel, name="row", out_shape=inside(piece), in_specs=[vmem] * ROW, out_specs=vmem
    )(*near(pieces))
    rows = [shifted(row, step_z=k) for k in (1, 2, 3)]
    enter = jax.ShapeDtypeStruct((n, pw), BF)
    enters = pl.pallas_call(
        enter_kernel,
        name="enter",
        out_shape=[inside(enter)] * ROW,
        in_specs=[vmem] * (ROW + 3),
        out_specs=[vmem] * ROW,
        scratch_shapes=[
            pltpu.VMEM((ROW, n, pw), BF),
            pltpu.VMEM((ROW, 8, pw), F32),
            pltpu.VMEM((ROW, n, pw), BF),
        ],
    )(*near(pieces + rows))
    enters = along_row(enters)
    enter_shapes = [pltpu.VMEM((n, early_width), BF), pltpu.VMEM((n, width - early_width), BF)]
    enter_early, enter_late, give = pl.pallas_call(
        split_kernel,
        name="split",
        out_shape=enter_shapes + [pltpu.VMEM((n, half), BF)],
        in_specs=[vmem] * (ROW + 1),
        out_specs=[vmem] * 3,
        scratch_shapes=[pltpu.VMEM((ROW, n, pw), BF)],
    )(*near([earlier] + enters))
    got = shifted(give, swap=1)
    enter_early, enter_late = pl.pallas_call(
        sorted_kernel,
        name="sorted",
        out_shape=enter_shapes,
        in_specs=[vmem] * 3,
        out_specs=[vmem] * 2,
        input_output_aliases={1: 0, 2: 1},
    )(*near([got, enter_early, enter_late]))
    early_enters = over_all_docs(enter_early, -1)

    late_width = width - early_width
    late = pl.pallas_call(
        functools.partial(late_kernel, early),
        name="late",
        out_shape=pltpu.VMEM((tokens, late_width), BF),
        in_specs=[smem, vmem] + [anywhere] * 5,
        out_specs=vmem,
        scratch_shapes=[pltpu.VMEM((tokens, Q), BF)] + local_scratch(heads - early, 4),
    )(skip, *near([enter_late]), first, values, log_decay, b_in, c_in)
    lates = over_all_docs(late, 1)

    result = jax.ShapeDtypeStruct((doc_n * 2, Q, width), BF)
    owned = pl.pallas_call(
        finish_kernel,
        name="finish",
        out_shape=result,
        in_specs=[smem] + [anywhere] * 12,
        out_specs=anywhere,
        scratch_shapes=[
            pltpu.VMEM((doc_n,) + first.shape, BF),
            pltpu.VMEM((doc_n,) + other.shape, BF),
            pltpu.VMEM((doc_n,) + enter_early.shape, BF),
            pltpu.VMEM((doc_n, tokens, early_width), BF),
            pltpu.VMEM((Q, width), BF),
            dma((doc_n,)),
            dma((doc_n,)),
            dma((doc_n,)),
            dma((doc_n * 2,)),
            dma((doc_n * 2,)),
        ],
    )(owner, *far(firsts), *far(others), *far(early_enters))
    owned = pl.pallas_call(
        functools.partial(owned_kernel, early_width),
        name="owned",
        out_shape=result,
        in_specs=[smem] + [anywhere] * 5,
        out_specs=anywhere,
        scratch_shapes=[pltpu.VMEM((doc_n,) + late.shape, BF), dma((doc_n,)), dma((doc_n * 2,))],
        input_output_aliases={5: 0},
    )(owner, *far(lates), owned)
    return owned[None]


def solution(mesh):
    in_specs = (
        P("doc", "seq", None),
        P("doc", "seq", None),
        P("doc", "seq", None),
        P("doc", None, "seq"),
        P(),
        P(None, "seq"),
    )
    out_specs = P("doc", "seq", None, None)
    return jax.shard_map(whole, mesh=mesh, in_specs=in_specs, out_specs=out_specs, check_vma=False)
```

```python
import functools

import jax
import jax.numpy as jnp
from jax import lax
from jax.experimental import pallas as pl
from jax.experimental.pallas import tpu as pltpu
from jax.sharding import PartitionSpec as P

Q = 128
ROW = 4
CORES = 2
GH = 8
HDIM = 64
WIDE = 1024
EARLY = (16, 16)
LATE = (8, 24)
TAIL = 16
LOG2E = 1.4426950408889634
F32 = jnp.float32
BF = jnp.bfloat16


def iota(shape, dim):
    return lax.broadcasted_iota(jnp.int32, shape, dim)


def dot(a, b, ca=1, cb=0):
    return lax.dot_general(a, b, (((ca,), (cb,)), ((), ())), preferred_element_type=F32)


def core_at():
    return lax.rem(lax.axis_index("seq"), CORES)


def row_at():
    return lax.rem(lax.div(lax.axis_index("seq"), CORES), ROW)


def level_at():
    return lax.div(lax.axis_index("seq"), CORES * ROW)


def half_of(heads, own):
    core = core_at() if own else CORES - 1 - core_at()
    return pl.multiple_of(core * (heads // CORES), heads // CORES)


def thirds(x):
    hi = x.astype(BF)
    rest = x - hi.astype(F32)
    mid = rest.astype(BF)
    lo = (rest - mid.astype(F32)).astype(BF)
    return hi, mid, lo


def triangle(n, strict_upper=False):
    rows, cols = iota((n, n), 0), iota((n, n), 1)
    keep = cols > rows if strict_upper else cols <= rows
    return jnp.where(keep, 1.0, 0.0).astype(BF)


def summed(weights, log_decay):
    heads = log_decay.shape[0]
    parts = jnp.concatenate([p.astype(F32) for p in thirds(log_decay)], axis=0).astype(BF)
    sums = dot(weights, parts, 1, 1)
    return sums[:, 0:heads] + sums[:, heads : 2 * heads] + sums[:, 2 * heads : 3 * heads]


def states_kernel(values_at, decay_at, b_at, mine, other, values, log_decay, b_in, pick, held, sems):
    tokens, width = values.shape
    wait = bring(((decay_at, log_decay), (b_at, b_in)), values_at, 0, values, WIDE, sems)
    n = b_in.shape[1]
    count = WIDE // HDIM
    steps = width // WIDE
    core = core_at()
    shape = pick.shape
    head = jnp.bitwise_and(iota(shape, 0), count - 1)
    keep = (head == lax.shift_right_logical(iota(shape, 1), HDIM.bit_length() - 1)) & (iota(shape, 0) < 3 * count)
    pick[...] = jnp.where(keep, 1.0, 0.0).astype(BF)
    wait()
    weights = jnp.concatenate([triangle(tokens, True), jnp.ones((TAIL, tokens), BF)], axis=0)
    parts = [p.astype(F32) for p in thirds(summed(weights, log_decay[...] * LOG2E))]
    for i in range(steps):
        cut = [p[:, i * count : (i + 1) * count] for p in parts]
        code = jnp.concatenate(cut + [jnp.zeros_like(cut[0])], axis=1).astype(BF)
        wide = dot(code, pick[...])
        wait(i)
        vals = values[:, i * WIDE : (i + 1) * WIDE].astype(F32)
        scaled = (vals * jnp.exp2(wide[0:tokens])).astype(BF)
        half, at = i * WIDE // mine.shape[1], i * WIDE % mine.shape[1]
        held[half, 0:n, at : at + WIDE] = dot(b_in[...], scaled, 0, 0).astype(BF)
        held[half, n:, at : at + WIDE] = tail_of(wide[tokens : tokens + 1])
    mine[...] = held[core]
    other[...] = held[1 - core]


def chip_kernel(mine, theirs, *refs):
    outs, earlier, held = refs[:-2], refs[-2], refs[-1]
    n, pw = outs[0].shape[0] - TAIL, outs[0].shape[1]
    core = core_at()
    for g in range(ROW):
        at = slice(g * pw, (g + 1) * pw)
        a, b = mine[0:n, at].astype(F32), theirs[0:n, at].astype(F32)
        ta, tb = tail_total(mine, n, at), tail_total(theirs, n, at)
        state = jnp.where(core == 0, jnp.exp2(tb), 1.0) * a + jnp.where(core == 0, 1.0, jnp.exp2(ta)) * b
        slot = lax.rem(g - row_at() + ROW, ROW)
        held[slot, 0:n, :] = state.astype(BF)
        held[slot, n:, :] = tail_of(ta + tb)
    for k, out in enumerate(outs):
        out[...] = held[k]

    @pl.when(core == 0)
    def _():
        earlier[...] = mine[...]

    @pl.when(core != 0)
    def _():
        earlier[...] = theirs[...]


def tail_total(piece, n, lanes):
    tail = piece[n : n + TAIL, lanes].astype(F32)
    return tail[0:1] + tail[1:2] + tail[2:3]


def tail_of(total):
    hi, mid, lo = thirds(total)
    row = iota((TAIL, total.shape[1]), 0)
    tail = jnp.where(row == 0, hi.astype(F32), jnp.where(row == 1, mid.astype(F32), lo.astype(F32)))
    return tail.astype(BF)


def total_of(piece, n):
    tail = piece[n : n + TAIL, :].astype(F32)
    return tail[0:1] + tail[1:2] + tail[2:3]


def row_kernel(*refs):
    pieces, out = refs[:-1], refs[-1]
    n = out.shape[0] - TAIL
    me = row_at()
    where = [lax.rem(me - k + ROW, ROW) for k in range(ROW)]
    totals = [total_of(p, n) for p in pieces]
    acc = jnp.zeros((n, out.shape[1]), F32)
    for k in range(ROW):
        later = jnp.zeros_like(totals[0])
        for j in range(ROW):
            if j != k:
                later = later + jnp.where(where[j] > where[k], totals[j], 0.0)
        acc = acc + jnp.exp2(later) * pieces[k][0:n, :].astype(F32)
    total = totals[0]
    for j in range(1, ROW):
        total = total + totals[j]
    out[0:n, :] = acc.astype(BF)
    out[n:, :] = tail_of(total)


def enter_kernel(*refs):
    pieces, rows = refs[:ROW], refs[ROW : ROW + 3]
    outs, held, totals, sent = refs[ROW + 3 : 2 * ROW + 3], refs[-3], refs[-2], refs[-1]
    n = outs[0].shape[0]
    me = row_at()
    for k in range(ROW):
        slot = lax.rem(me - k + ROW, ROW)
        held[slot] = pieces[k][0:n, :]
        totals[slot] = jnp.broadcast_to(total_of(pieces[k], n), totals.shape[1:])
    one, two, three = rows
    level = level_at()
    near = total_of(one, n)
    zero = jnp.zeros_like(near)
    enter = jnp.where(level > 0, zero + 1.0, zero) * one[0:n, :].astype(F32)
    enter = enter + jnp.where(level > 1, jnp.exp2(near), zero) * two[0:n, :].astype(F32)
    near = near + total_of(two, n)
    enter = enter + jnp.where(level > 2, jnp.exp2(near), zero) * three[0:n, :].astype(F32)
    for q in range(ROW):
        sent[lax.rem(q - me + ROW, ROW)] = enter.astype(BF)
        if q + 1 < ROW:
            enter = jnp.exp2(totals[q][0:1]) * enter + held[q].astype(F32)
    for k in range(ROW):
        outs[k][...] = sent[k]


def token_sums(lower, log_decay):
    heads = log_decay.shape[0]
    parts = jnp.concatenate([p.astype(F32) for p in thirds(log_decay * LOG2E)], axis=0).astype(BF)
    sums = dot(lower, parts, 1, 1)
    line = dot(parts, lower, 1, 1)
    return (
        sums[:, 0:heads] + sums[:, heads : 2 * heads] + sums[:, 2 * heads : 3 * heads],
        line[0:heads] + line[heads : 2 * heads] + line[2 * heads : 3 * heads],
    )


def local_part(skip, first_head, vals, sums, line, scores, emit):
    tokens, width = vals.shape
    hdim = width // GH
    blocks = tokens // Q
    keep = iota((Q, Q), 0) >= iota((Q, Q), 1)
    lanes = iota((Q, 2 * hdim), 1) < hdim
    for pair in range(GH // 2):
        col = slice(pair * 2 * hdim, (pair + 1) * 2 * hdim)
        mine = vals[:, col]
        halves = [
            [jnp.where(lanes, mine[j * Q : (j + 1) * Q], 0).astype(BF) for j in range(blocks)],
            [jnp.where(lanes, 0, mine[j * Q : (j + 1) * Q]).astype(BF) for j in range(blocks)],
        ]
        gain = jnp.where(lanes[0:1], skip[first_head + 2 * pair], skip[first_head + 2 * pair + 1])
        for i in range(blocks):
            left, right = [], []
            for side in range(2):
                head = 2 * pair + side
                column = jnp.broadcast_to(sums[i * Q : (i + 1) * Q, head : head + 1], (Q, Q))
                for j in range(i + 1):
                    gap = column - line[head : head + 1, j * Q : (j + 1) * Q]
                    if i == j:
                        gap = jnp.where(keep, gap, -1e30)
                    here = scores[i * Q : (i + 1) * Q, j * Q : (j + 1) * Q]
                    left.append((here * jnp.exp2(gap)).astype(BF))
                    right.append(halves[side][j])
            acc = dot(jnp.concatenate(left, axis=1), jnp.concatenate(right, axis=0))
            emit(i, pair * 2 * hdim, acc + gain * mine[i * Q : (i + 1) * Q].astype(F32))


def bring(small, values_at, first_lane, values, width, sems):
    n = len(small)
    copies = [pltpu.make_async_copy(x, y, sems.at[i]) for i, (x, y) in enumerate(small)]

    def lanes(i):
        at = pl.multiple_of(first_lane + i * width, width)
        return pltpu.make_async_copy(
            values_at.at[:, pl.ds(at, width)], values.at[:, i * width : (i + 1) * width], sems.at[n + i]
        )

    for copy in copies:
        copy.start()
    for i in range(values.shape[1] // width):
        lanes(i).start()

    def wait(i=None):
        if i is not None:
            lanes(i).wait()
            return
        for copy in copies:
            copy.wait()

    return wait


def local_groups(start, skip, values, sums, line, scores, emit, wait):
    width = GH * HDIM
    for i in range(values.shape[1] // width):
        wait(i)
        heads = slice(i * GH, (i + 1) * GH)

        def put(block, lane, x):
            emit(block, i * width + lane, x)

        vals = values[:, i * width : (i + 1) * width]
        local_part(skip, start + i * GH, vals, sums[:, heads], line[heads], scores, put)


def with_lanes(x):
    return jnp.concatenate([x, jnp.zeros((x.shape[0], Q - x.shape[1]), F32)], axis=1).astype(BF)


def prepared(start, own, count, values_at, decay_at, b_at, c_at, values, log_decay, b_in, c_in, lower, scores, sems):
    first = half_of(log_decay.shape[0], own) + start
    small = ((decay_at, log_decay), (b_at, b_in), (c_at, c_in))
    wait = bring(small, values_at, first * HDIM, values, GH * HDIM, sems)
    lower[...] = triangle(values.shape[0])
    wait()
    scores[...] = dot(c_in[...], b_in[...], 1, 1)
    sums, line = token_sums(lower[...], log_decay[pl.ds(pl.multiple_of(first, GH), count), :])
    return first, sums, line, wait


def first_local_kernel(skip, values_at, decay_at, b_at, c_at, out, values, log_decay, b_in, c_in, lower, scores, sems):
    ends = out.shape[1] - 2 * Q
    arrays = (values_at, decay_at, b_at, c_at, values, log_decay, b_in, c_in, lower, scores, sems)
    first, sums, line, wait = prepared(0, True, log_decay.shape[0] // CORES, *arrays)
    out[:, ends : ends + Q] = c_in[...]
    out[:, ends + Q :] = with_lanes(jnp.exp2(sums))

    def emit(i, at, x):
        out[i * Q : (i + 1) * Q, at : at + x.shape[1]] = x.astype(BF)

    local_groups(first, skip, values, sums, line, scores, emit, wait)


def other_local_kernel(start, skip, values_at, decay_at, b_at, c_at, out, *scratch):
    values, scores = scratch[0], scratch[-2]
    count = values.shape[1] // HDIM
    first, sums, line, wait = prepared(start, True, count, values_at, decay_at, b_at, c_at, *scratch)

    def emit(i, at, x):
        out[i * Q : (i + 1) * Q, at : at + x.shape[1]] = x.astype(BF)

    local_groups(first, skip, values, sums, line, scores, emit, wait)


def late_kernel(start, skip, enter, values_at, decay_at, b_at, c_at, out, *scratch):
    values, c_in, scores = scratch[0], scratch[3], scratch[-2]
    count = values.shape[1] // HDIM
    first, sums, line, wait = prepared(start, False, count, values_at, decay_at, b_at, c_at, *scratch)
    decays = with_lanes(jnp.exp2(sums))
    row = iota((Q, Q), 0)
    side = lax.shift_right_logical(iota((Q, Q), 1), HDIM.bit_length() - 1)

    def emit(i, at, x):
        pick = jnp.where(row == side + at // HDIM, 1.0, 0.0).astype(BF)
        rows = slice(i * Q, (i + 1) * Q)
        lane = start * HDIM + at
        add = dot(decays[rows], pick) * dot(c_in[rows, :], enter[:, lane : lane + Q])
        out[rows, at : at + Q] = (x + add).astype(BF)

    local_groups(first, skip, values, sums, line, scores, emit, wait)


def split_kernel(earlier, *refs):
    enters, keep, give, held = refs[:ROW], refs[ROW], refs[ROW + 1], refs[ROW + 2]
    n, pw = enters[0].shape
    core = core_at()
    for k in range(ROW):
        held[lax.rem(row_at() - k + ROW, ROW)] = enters[k][...]

    def emit(before, after):
        for g in range(ROW):
            at = slice(g * pw, (g + 1) * pw)
            enter = held[g]
            decay = jnp.exp2(tail_total(earlier, n, at))
            before[:, at] = enter
            after[:, at] = (decay * enter.astype(F32) + earlier[0:n, at].astype(F32)).astype(BF)

    @pl.when(core == 0)
    def _():
        emit(keep, give)

    @pl.when(core != 0)
    def _():
        emit(give, keep)


def owned_plan(owner, docs):
    me = lax.axis_index("doc")
    plans = []
    for r in range(docs):
        doc = lax.rem(me + r, docs)
        first, second = owner[doc, 0] == me, owner[doc, 1] == me
        plans.append((doc, first, second))
    return plans


def write_owned(plan, r, rows, out, lanes, sems, zeros=None, act="start"):
    doc, first, second = plan
    both = jnp.logical_and(first, second)

    def go(when, source, to, i):
        @pl.when(when)
        def _():
            copy = pltpu.make_async_copy(source, out.at[to, :, lanes], sems.at[2 * r + i])
            copy.start() if act == "start" else copy.wait()

    if rows is not None:
        go(first, rows.at[0:Q], 2 * doc, 0)
        go(jnp.logical_and(jnp.logical_not(first), second), rows.at[Q : 2 * Q], 2 * doc, 0)
        go(both, rows.at[Q : 2 * Q], 2 * doc + 1, 1)
    if zeros is not None:
        go(jnp.logical_not(jnp.logical_or(first, second)), zeros, 2 * doc, 0)
        go(jnp.logical_not(both), zeros, 2 * doc + 1, 1)


def read_part(sources, r, target, sems, act="start"):
    copy = pltpu.make_async_copy(sources[r], target.at[r], sems.at[r])
    copy.start() if act == "start" else copy.wait()


def finish_kernel(owner, *refs):
    firsts, others, enters = refs[0:4], refs[4:8], refs[8:12]
    out, first, other, enter, done, zeros, s_first, s_other, s_enter, s_out, s_zero = refs[12:]
    plans = owned_plan(owner, 4)
    groups = ((firsts, first, s_first), (others, other, s_other), (enters, enter, s_enter))
    lanes = pl.ds(pl.multiple_of(core_at() * done.shape[2], done.shape[2]), done.shape[2])

    def some(plan):
        return jnp.logical_or(plan[1], plan[2])

    for r, plan in enumerate(plans):

        @pl.when(some(plan))
        def _():
            for sources, target, sems in groups:
                read_part(sources, r, target, sems)

    zeros[...] = jnp.zeros_like(zeros)
    for r, plan in enumerate(plans):
        write_owned(plan, r, None, out, pl.ds(0, zeros.shape[1]), s_zero, zeros)

    ends = first.shape[2] - 2 * Q
    step = 512
    for r, plan in enumerate(plans):

        @pl.when(some(plan))
        def _():
            for sources, target, sems in groups:
                read_part(sources, r, target, sems, "wait")
            c = first[r, :, ends : ends + Q]
            decay = first[r, :, ends + Q :]
            for at in range(0, done.shape[2], step):
                head = iota((Q, step), 0)
                pick = jnp.where(head == (iota((Q, step), 1) + at) // HDIM, 1.0, 0.0).astype(BF)
                add = dot(decay, pick) * dot(c, enter[r, :, at : at + step])
                here = first[r, :, at : at + step] if at < ends else other[r, :, at - ends : at - ends + step]
                done[r, :, at : at + step] = (here.astype(F32) + add).astype(BF)

        write_owned(plan, r, done.at[r], out, lanes, s_out)
    for r, plan in enumerate(plans):
        write_owned(plan, r, done.at[r], out, lanes, s_out, None, "wait")
        write_owned(plan, r, None, out, pl.ds(0, zeros.shape[1]), s_zero, zeros, "wait")


def owned_kernel(start, which, owner, *refs):
    out, held, s_in, s_out = refs[-4:]
    plans = owned_plan(owner, 4)
    width = refs[0].shape[1]
    half = out.shape[2] // CORES
    lane = (CORES - 1 - core_at()) * half + start * HDIM
    lanes = pl.ds(pl.multiple_of(lane, GH * HDIM), width)
    if isinstance(which, int):
        for act in ("start", "wait"):
            write_owned(plans[which], which, refs[0], out, lanes, s_out, None, act)
        return
    sources = dict(zip(which, refs))
    for act in ("start", "wait"):
        for r in which:
            plan = plans[r]

            @pl.when(jnp.logical_or(plan[1], plan[2]))
            def _():
                read_part(sources, r, held, s_in, act)

            if act == "wait":
                write_owned(plan, r, held.at[r], out, lanes, s_out)
    for r in which:
        write_owned(plans[r], r, held.at[r], out, lanes, s_out, None, "wait")


def inside(shape):
    return pltpu.VMEM(shape.shape, shape.dtype)


def near(arrays):
    return [pltpu.with_memory_space_constraint(x, pltpu.VMEM) for x in arrays]


def far(arrays):
    return [pltpu.with_memory_space_constraint(x, pltpu.HBM) for x in arrays]


def whole(values, b_in, c_in, log_decay, skip, owner):
    seq_n = lax.axis_size("seq")
    doc_n = lax.axis_size("doc")
    per_level = ROW * CORES
    levels = seq_n // per_level
    values, b_in, c_in, log_decay = values[0], b_in[0], c_in[0], log_decay[0]
    tokens, width = values.shape
    heads = log_decay.shape[0]
    n = b_in.shape[1]

    def shifted(x, step_x=0, step_z=0, swap=0):
        pairs = []
        for i in range(seq_n):
            z, at, core = i // per_level, i % per_level // CORES, i % CORES
            z, at, core = (z + step_z) % levels, (at + step_x) % ROW, (core + swap) % CORES
            pairs.append((i, z * per_level + at * CORES + core))
        return lax.ppermute(x, "seq", pairs)

    def along_row(pieces):
        return [pieces[0]] + [shifted(pieces[k], step_x=k) for k in range(1, ROW)]

    def over_docs(x, k):
        return lax.ppermute(x, "doc", [(d, (d + k) % doc_n) for d in range(doc_n)])

    def over_all_docs(x, far_by):
        before = over_docs(x, 1)
        after = over_docs(x, doc_n - 1)
        far = over_docs(before, 1) if far_by > 0 else over_docs(after, doc_n - 1)
        return [x, after, far, before]

    smem = pl.BlockSpec(memory_space=pltpu.SMEM)
    vmem = pl.BlockSpec(memory_space=pltpu.VMEM)
    anywhere = pl.BlockSpec(memory_space=pl.ANY)

    first_width = EARLY[0] * HDIM
    dma = pltpu.SemaphoreType.DMA

    def local_scratch(count, small=3):
        return [
            pltpu.VMEM((tokens, count * HDIM), BF),
            pltpu.VMEM((heads, tokens), F32),
            pltpu.VMEM((tokens, n), BF),
            pltpu.VMEM((tokens, n), BF),
            pltpu.VMEM((tokens, tokens), BF),
            pltpu.VMEM((tokens, tokens), F32),
            dma((small + count // GH,)),
        ]

    first = pl.pallas_call(
        first_local_kernel,
        name="local_first",
        out_shape=jax.ShapeDtypeStruct((tokens, first_width + 2 * Q), BF),
        in_specs=[smem] + [anywhere] * 4,
        out_specs=vmem,
        scratch_shapes=local_scratch(EARLY[0]),
    )(skip, values, log_decay, b_in, c_in)
    firsts = over_all_docs(first, -1)

    half = width // CORES
    pw = half // ROW
    half_shape = jax.ShapeDtypeStruct((n + TAIL, half), BF)
    piece = jax.ShapeDtypeStruct((n + TAIL, pw), BF)
    mine, other_half = pl.pallas_call(
        states_kernel,
        name="states",
        out_shape=[inside(half_shape)] * 2,
        in_specs=[anywhere] * 3,
        out_specs=[vmem] * 2,
        scratch_shapes=[
            pltpu.VMEM((tokens, width), BF),
            pltpu.VMEM((heads, tokens), F32),
            pltpu.VMEM((tokens, n), BF),
            pltpu.VMEM((4 * WIDE // HDIM, WIDE), BF),
            pltpu.VMEM((CORES,) + half_shape.shape, BF),
            dma((2 + width // WIDE,)),
        ],
    )(values, log_decay, b_in)
    theirs = shifted(other_half, swap=1)
    *pieces, earlier = pl.pallas_call(
        chip_kernel,
        name="chip",
        out_shape=[inside(piece)] * ROW + [inside(half_shape)],
        in_specs=[vmem, vmem],
        out_specs=[vmem] * (ROW + 1),
        scratch_shapes=[pltpu.VMEM((ROW,) + piece.shape, BF)],
    )(*near([mine, theirs]))
    pieces = along_row(pieces)

    other = pl.pallas_call(
        functools.partial(other_local_kernel, EARLY[0]),
        name="local_other",
        out_shape=jax.ShapeDtypeStruct((tokens, EARLY[1] * HDIM), BF),
        in_specs=[smem] + [anywhere] * 4,
        out_specs=vmem,
        scratch_shapes=local_scratch(EARLY[1]),
    )(skip, values, log_decay, b_in, c_in)
    others = over_all_docs(other, 1)

    row = pl.pallas_call(
        row_kernel, name="row", out_shape=inside(piece), in_specs=[vmem] * ROW, out_specs=vmem
    )(*near(pieces))
    rows = [shifted(row, step_z=k) for k in (1, 2, 3)]
    enter = jax.ShapeDtypeStruct((n, pw), BF)
    enters = pl.pallas_call(
        enter_kernel,
        name="enter",
        out_shape=[inside(enter)] * ROW,
        in_specs=[vmem] * (ROW + 3),
        out_specs=[vmem] * ROW,
        scratch_shapes=[
            pltpu.VMEM((ROW, n, pw), BF),
            pltpu.VMEM((ROW, 8, pw), F32),
            pltpu.VMEM((ROW, n, pw), BF),
        ],
    )(*near(pieces + rows))
    enters = along_row(enters)
    keep, give = pl.pallas_call(
        split_kernel,
        name="split",
        out_shape=[pltpu.VMEM((n, half), BF)] * 2,
        in_specs=[vmem] * (ROW + 1),
        out_specs=[vmem] * 2,
        scratch_shapes=[pltpu.VMEM((ROW, n, pw), BF)],
    )(*near([earlier] + enters))
    got = shifted(give, swap=1)
    early_enters = over_all_docs(keep, -1)

    lates = []
    start = 0
    for i, count in enumerate(LATE):
        late = pl.pallas_call(
            functools.partial(late_kernel, start),
            out_shape=pltpu.VMEM((tokens, count * HDIM), BF),
            in_specs=[smem, vmem] + [anywhere] * 4,
            out_specs=vmem,
            scratch_shapes=local_scratch(count),
        )(skip, *near([got]), values, log_decay, b_in, c_in)
        lates.append((start, over_all_docs(late, -1 if i == 0 else 1)))
        start += count

    result = jax.ShapeDtypeStruct((doc_n * 2, Q, width), BF)
    owned = pl.pallas_call(
        finish_kernel,
        name="finish",
        out_shape=result,
        in_specs=[smem] + [anywhere] * 12,
        out_specs=anywhere,
        scratch_shapes=[
            pltpu.VMEM((doc_n,) + first.shape, BF),
            pltpu.VMEM((doc_n,) + other.shape, BF),
            pltpu.VMEM((doc_n,) + keep.shape, BF),
            pltpu.VMEM((doc_n, tokens, half), BF),
            pltpu.VMEM((Q, width), BF),
            dma((doc_n,)),
            dma((doc_n,)),
            dma((doc_n,)),
            dma((doc_n * 2,)),
            dma((doc_n * 2,)),
        ],
    )(owner, *far(firsts), *far(others), *far(early_enters))

    def write_late(owned, i, which):
        start, arrays = lates[i]
        if isinstance(which, int):
            arrays = near([arrays[which]])
        else:
            arrays = far([arrays[r] for r in which])
        return pl.pallas_call(
            functools.partial(owned_kernel, start, which),
            out_shape=result,
            in_specs=[smem] + [vmem if len(arrays) == 1 else anywhere] * len(arrays) + [anywhere],
            out_specs=anywhere,
            scratch_shapes=[
                pltpu.VMEM((doc_n,) + arrays[0].shape, BF),
                dma((doc_n,)),
                dma((doc_n * 2,)),
            ],
            input_output_aliases={1 + len(arrays): 0},
        )(owner, *arrays, owned)

    near_docs, far_doc = (0, 1, 3), 2
    for i in range(len(LATE)):
        owned = write_late(owned, i, near_docs)
    for i in range(len(LATE)):
        owned = write_late(owned, i, far_doc)
    return owned[None]


def solution(mesh):
    in_specs = (
        P("doc", "seq", None),
        P("doc", "seq", None),
        P("doc", "seq", None),
        P("doc", None, "seq"),
        P(),
        P(None, "seq"),
    )
    out_specs = P("doc", "seq", None, None)
    return jax.shard_map(whole, mesh=mesh, in_specs=in_specs, out_specs=out_specs, check_vma=False)
```

```python
import functools

import jax
import jax.numpy as jnp
from jax import lax
from jax.experimental import pallas as pl
from jax.experimental.pallas import tpu as pltpu
from jax.sharding import PartitionSpec as P

Q = 128
ROW = 4
CORES = 2
GH = 8
HDIM = 64
WIDE = 1024
EARLY = (16, 16)
LATE = (24, 8)
TAIL = 16
LOG2E = 1.4426950408889634
F32 = jnp.float32
BF = jnp.bfloat16


def iota(shape, dim):
    return lax.broadcasted_iota(jnp.int32, shape, dim)


def dot(a, b, ca=1, cb=0):
    return lax.dot_general(a, b, (((ca,), (cb,)), ((), ())), preferred_element_type=F32)


def core_at():
    return lax.rem(lax.axis_index("seq"), CORES)


def row_at():
    return lax.rem(lax.div(lax.axis_index("seq"), CORES), ROW)


def level_at():
    return lax.div(lax.axis_index("seq"), CORES * ROW)


def half_of(heads, own):
    core = core_at() if own else CORES - 1 - core_at()
    return pl.multiple_of(core * (heads // CORES), heads // CORES)


def thirds(x):
    hi = x.astype(BF)
    rest = x - hi.astype(F32)
    mid = rest.astype(BF)
    lo = (rest - mid.astype(F32)).astype(BF)
    return hi, mid, lo


def triangle(n, strict_upper=False):
    rows, cols = iota((n, n), 0), iota((n, n), 1)
    keep = cols > rows if strict_upper else cols <= rows
    return jnp.where(keep, 1.0, 0.0).astype(BF)


def summed(weights, log_decay):
    heads = log_decay.shape[0]
    parts = jnp.concatenate([p.astype(F32) for p in thirds(log_decay)], axis=0).astype(BF)
    sums = dot(weights, parts, 1, 1)
    return sums[:, 0:heads] + sums[:, heads : 2 * heads] + sums[:, 2 * heads : 3 * heads]


def states_kernel(values_at, decay_at, b_at, mine, other, values, log_decay, b_in, pick, held, sems):
    tokens, width = values.shape
    wait = bring(((decay_at, log_decay), (b_at, b_in)), values_at, 0, values, WIDE, sems)
    n = b_in.shape[1]
    count = WIDE // HDIM
    steps = width // WIDE
    core = core_at()
    shape = pick.shape
    head = jnp.bitwise_and(iota(shape, 0), count - 1)
    keep = (head == lax.shift_right_logical(iota(shape, 1), HDIM.bit_length() - 1)) & (iota(shape, 0) < 3 * count)
    pick[...] = jnp.where(keep, 1.0, 0.0).astype(BF)
    wait()
    weights = jnp.concatenate([triangle(tokens, True), jnp.ones((TAIL, tokens), BF)], axis=0)
    parts = [p.astype(F32) for p in thirds(summed(weights, log_decay[...] * LOG2E))]
    for i in range(steps):
        cut = [p[:, i * count : (i + 1) * count] for p in parts]
        code = jnp.concatenate(cut + [jnp.zeros_like(cut[0])], axis=1).astype(BF)
        wide = dot(code, pick[...])
        wait(i)
        vals = values[:, i * WIDE : (i + 1) * WIDE].astype(F32)
        scaled = (vals * jnp.exp2(wide[0:tokens])).astype(BF)
        half, at = i * WIDE // mine.shape[1], i * WIDE % mine.shape[1]
        held[half, 0:n, at : at + WIDE] = dot(b_in[...], scaled, 0, 0).astype(BF)
        held[half, n:, at : at + WIDE] = tail_of(wide[tokens : tokens + 1])
    mine[...] = held[core]
    other[...] = held[1 - core]


def chip_kernel(mine, theirs, *refs):
    outs, earlier, held = refs[:-2], refs[-2], refs[-1]
    n, pw = outs[0].shape[0] - TAIL, outs[0].shape[1]
    core = core_at()
    for g in range(ROW):
        at = slice(g * pw, (g + 1) * pw)
        a, b = mine[0:n, at].astype(F32), theirs[0:n, at].astype(F32)
        ta, tb = tail_total(mine, n, at), tail_total(theirs, n, at)
        state = jnp.where(core == 0, jnp.exp2(tb), 1.0) * a + jnp.where(core == 0, 1.0, jnp.exp2(ta)) * b
        slot = lax.rem(g - row_at() + ROW, ROW)
        held[slot, 0:n, :] = state.astype(BF)
        held[slot, n:, :] = tail_of(ta + tb)
    for k, out in enumerate(outs):
        out[...] = held[k]

    @pl.when(core == 0)
    def _():
        earlier[...] = mine[...]

    @pl.when(core != 0)
    def _():
        earlier[...] = theirs[...]


def tail_total(piece, n, lanes):
    tail = piece[n : n + TAIL, lanes].astype(F32)
    return tail[0:1] + tail[1:2] + tail[2:3]


def tail_of(total):
    hi, mid, lo = thirds(total)
    row = iota((TAIL, total.shape[1]), 0)
    tail = jnp.where(row == 0, hi.astype(F32), jnp.where(row == 1, mid.astype(F32), lo.astype(F32)))
    return tail.astype(BF)


def total_of(piece, n):
    tail = piece[n : n + TAIL, :].astype(F32)
    return tail[0:1] + tail[1:2] + tail[2:3]


def row_kernel(*refs):
    pieces, out = refs[:-1], refs[-1]
    n = out.shape[0] - TAIL
    me = row_at()
    where = [lax.rem(me - k + ROW, ROW) for k in range(ROW)]
    totals = [total_of(p, n) for p in pieces]
    acc = jnp.zeros((n, out.shape[1]), F32)
    for k in range(ROW):
        later = jnp.zeros_like(totals[0])
        for j in range(ROW):
            if j != k:
                later = later + jnp.where(where[j] > where[k], totals[j], 0.0)
        acc = acc + jnp.exp2(later) * pieces[k][0:n, :].astype(F32)
    total = totals[0]
    for j in range(1, ROW):
        total = total + totals[j]
    out[0:n, :] = acc.astype(BF)
    out[n:, :] = tail_of(total)


def enter_kernel(*refs):
    pieces, rows = refs[:ROW], refs[ROW : ROW + 3]
    outs, held, totals, sent = refs[ROW + 3 : 2 * ROW + 3], refs[-3], refs[-2], refs[-1]
    n = outs[0].shape[0]
    me = row_at()
    for k in range(ROW):
        slot = lax.rem(me - k + ROW, ROW)
        held[slot] = pieces[k][0:n, :]
        totals[slot] = jnp.broadcast_to(total_of(pieces[k], n), totals.shape[1:])
    one, two, three = rows
    level = level_at()
    near = total_of(one, n)
    zero = jnp.zeros_like(near)
    enter = jnp.where(level > 0, zero + 1.0, zero) * one[0:n, :].astype(F32)
    enter = enter + jnp.where(level > 1, jnp.exp2(near), zero) * two[0:n, :].astype(F32)
    near = near + total_of(two, n)
    enter = enter + jnp.where(level > 2, jnp.exp2(near), zero) * three[0:n, :].astype(F32)
    for q in range(ROW):
        sent[lax.rem(q - me + ROW, ROW)] = enter.astype(BF)
        if q + 1 < ROW:
            enter = jnp.exp2(totals[q][0:1]) * enter + held[q].astype(F32)
    for k in range(ROW):
        outs[k][...] = sent[k]


def token_sums(lower, log_decay):
    heads = log_decay.shape[0]
    parts = jnp.concatenate([p.astype(F32) for p in thirds(log_decay * LOG2E)], axis=0).astype(BF)
    sums = dot(lower, parts, 1, 1)
    line = dot(parts, lower, 1, 1)
    return (
        sums[:, 0:heads] + sums[:, heads : 2 * heads] + sums[:, 2 * heads : 3 * heads],
        line[0:heads] + line[heads : 2 * heads] + line[2 * heads : 3 * heads],
    )


def local_part(skip, first_head, vals, sums, line, scores, emit):
    tokens, width = vals.shape
    hdim = width // GH
    blocks = tokens // Q
    keep = iota((Q, Q), 0) >= iota((Q, Q), 1)
    lanes = iota((Q, 2 * hdim), 1) < hdim
    for pair in range(GH // 2):
        col = slice(pair * 2 * hdim, (pair + 1) * 2 * hdim)
        mine = vals[:, col]
        halves = [
            [jnp.where(lanes, mine[j * Q : (j + 1) * Q], 0).astype(BF) for j in range(blocks)],
            [jnp.where(lanes, 0, mine[j * Q : (j + 1) * Q]).astype(BF) for j in range(blocks)],
        ]
        gain = jnp.where(lanes[0:1], skip[first_head + 2 * pair], skip[first_head + 2 * pair + 1])
        for i in range(blocks):
            left, right = [], []
            for side in range(2):
                head = 2 * pair + side
                column = jnp.broadcast_to(sums[i * Q : (i + 1) * Q, head : head + 1], (Q, Q))
                for j in range(i + 1):
                    gap = column - line[head : head + 1, j * Q : (j + 1) * Q]
                    if i == j:
                        gap = jnp.where(keep, gap, -1e30)
                    here = scores[i * Q : (i + 1) * Q, j * Q : (j + 1) * Q]
                    left.append((here * jnp.exp2(gap)).astype(BF))
                    right.append(halves[side][j])
            acc = dot(jnp.concatenate(left, axis=1), jnp.concatenate(right, axis=0))
            emit(i, pair * 2 * hdim, acc + gain * mine[i * Q : (i + 1) * Q].astype(F32))


def bring(small, values_at, first_lane, values, width, sems):
    n = len(small)
    copies = [pltpu.make_async_copy(x, y, sems.at[i]) for i, (x, y) in enumerate(small)]

    def lanes(i):
        at = pl.multiple_of(first_lane + i * width, width)
        return pltpu.make_async_copy(
            values_at.at[:, pl.ds(at, width)], values.at[:, i * width : (i + 1) * width], sems.at[n + i]
        )

    for copy in copies:
        copy.start()
    for i in range(values.shape[1] // width):
        lanes(i).start()

    def wait(i=None):
        if i is not None:
            lanes(i).wait()
            return
        for copy in copies:
            copy.wait()

    return wait


def local_groups(start, skip, values, sums, line, scores, emit, wait):
    width = GH * HDIM
    for i in range(values.shape[1] // width):
        wait(i)
        heads = slice(i * GH, (i + 1) * GH)

        def put(block, lane, x):
            emit(block, i * width + lane, x)

        vals = values[:, i * width : (i + 1) * width]
        local_part(skip, start + i * GH, vals, sums[:, heads], line[heads], scores, put)


def with_lanes(x):
    return jnp.concatenate([x, jnp.zeros((x.shape[0], Q - x.shape[1]), F32)], axis=1).astype(BF)


def prepared(start, own, count, values_at, decay_at, b_at, c_at, values, log_decay, b_in, c_in, lower, scores, sems):
    first = half_of(log_decay.shape[0], own) + start
    small = ((decay_at, log_decay), (b_at, b_in), (c_at, c_in))
    wait = bring(small, values_at, first * HDIM, values, GH * HDIM, sems)
    lower[...] = triangle(values.shape[0])
    wait()
    scores[...] = dot(c_in[...], b_in[...], 1, 1)
    sums, line = token_sums(lower[...], log_decay[pl.ds(pl.multiple_of(first, GH), count), :])
    return first, sums, line, wait


def first_local_kernel(skip, values_at, decay_at, b_at, c_at, out, values, log_decay, b_in, c_in, lower, scores, sems):
    ends = out.shape[1] - 2 * Q
    arrays = (values_at, decay_at, b_at, c_at, values, log_decay, b_in, c_in, lower, scores, sems)
    first, sums, line, wait = prepared(0, True, log_decay.shape[0] // CORES, *arrays)
    out[:, ends : ends + Q] = c_in[...]
    out[:, ends + Q :] = with_lanes(jnp.exp2(sums))

    def emit(i, at, x):
        out[i * Q : (i + 1) * Q, at : at + x.shape[1]] = x.astype(BF)

    local_groups(first, skip, values, sums, line, scores, emit, wait)


def other_local_kernel(start, skip, values_at, decay_at, b_at, c_at, out, *scratch):
    values, scores = scratch[0], scratch[-2]
    count = values.shape[1] // HDIM
    first, sums, line, wait = prepared(start, True, count, values_at, decay_at, b_at, c_at, *scratch)

    def emit(i, at, x):
        out[i * Q : (i + 1) * Q, at : at + x.shape[1]] = x.astype(BF)

    local_groups(first, skip, values, sums, line, scores, emit, wait)


def late_kernel(start, skip, enter, values_at, decay_at, b_at, c_at, out, *scratch):
    values, c_in, scores = scratch[0], scratch[3], scratch[-2]
    count = values.shape[1] // HDIM
    first, sums, line, wait = prepared(start, False, count, values_at, decay_at, b_at, c_at, *scratch)
    decays = with_lanes(jnp.exp2(sums))
    row = iota((Q, Q), 0)
    side = lax.shift_right_logical(iota((Q, Q), 1), HDIM.bit_length() - 1)

    def emit(i, at, x):
        pick = jnp.where(row == side + at // HDIM, 1.0, 0.0).astype(BF)
        rows = slice(i * Q, (i + 1) * Q)
        lane = start * HDIM + at
        add = dot(decays[rows], pick) * dot(c_in[rows, :], enter[:, lane : lane + Q])
        out[rows, at : at + Q] = (x + add).astype(BF)

    local_groups(first, skip, values, sums, line, scores, emit, wait)


def split_kernel(earlier, *refs):
    enters, keep, give, held = refs[:ROW], refs[ROW], refs[ROW + 1], refs[ROW + 2]
    n, pw = enters[0].shape
    core = core_at()
    for k in range(ROW):
        held[lax.rem(row_at() - k + ROW, ROW)] = enters[k][...]

    def emit(before, after):
        for g in range(ROW):
            at = slice(g * pw, (g + 1) * pw)
            enter = held[g]
            decay = jnp.exp2(tail_total(earlier, n, at))
            before[:, at] = enter
            after[:, at] = (decay * enter.astype(F32) + earlier[0:n, at].astype(F32)).astype(BF)

    @pl.when(core == 0)
    def _():
        emit(keep, give)

    @pl.when(core != 0)
    def _():
        emit(give, keep)


def owned_plan(owner, docs):
    me = lax.axis_index("doc")
    plans = []
    for r in range(docs):
        doc = lax.rem(me + r, docs)
        first, second = owner[doc, 0] == me, owner[doc, 1] == me
        plans.append((doc, first, second))
    return plans


def write_owned(plan, r, rows, out, lanes, sems, zeros=None, act="start"):
    doc, first, second = plan
    both = jnp.logical_and(first, second)

    def go(when, source, to, i):
        @pl.when(when)
        def _():
            copy = pltpu.make_async_copy(source, out.at[to, :, lanes], sems.at[2 * r + i])
            copy.start() if act == "start" else copy.wait()

    if rows is not None:
        go(first, rows.at[0:Q], 2 * doc, 0)
        go(jnp.logical_and(jnp.logical_not(first), second), rows.at[Q : 2 * Q], 2 * doc, 0)
        go(both, rows.at[Q : 2 * Q], 2 * doc + 1, 1)
    if zeros is not None:
        go(jnp.logical_not(jnp.logical_or(first, second)), zeros, 2 * doc, 0)
        go(jnp.logical_not(both), zeros, 2 * doc + 1, 1)


def read_part(sources, r, target, sems, act="start"):
    copy = pltpu.make_async_copy(sources[r], target.at[r], sems.at[r])
    copy.start() if act == "start" else copy.wait()


def finish_kernel(owner, *refs):
    firsts, others, enters = refs[0:4], refs[4:8], refs[8:12]
    out, first, other, enter, done, zeros, s_first, s_other, s_enter, s_out, s_zero = refs[12:]
    plans = owned_plan(owner, 4)
    groups = ((firsts, first, s_first), (others, other, s_other), (enters, enter, s_enter))
    lanes = pl.ds(pl.multiple_of(core_at() * done.shape[2], done.shape[2]), done.shape[2])

    def some(plan):
        return jnp.logical_or(plan[1], plan[2])

    for r, plan in enumerate(plans):

        @pl.when(some(plan))
        def _():
            for sources, target, sems in groups:
                read_part(sources, r, target, sems)

    zeros[...] = jnp.zeros_like(zeros)
    for r, plan in enumerate(plans):
        write_owned(plan, r, None, out, pl.ds(0, zeros.shape[1]), s_zero, zeros)

    ends = first.shape[2] - 2 * Q
    step = 512
    for r, plan in enumerate(plans):

        @pl.when(some(plan))
        def _():
            for sources, target, sems in groups:
                read_part(sources, r, target, sems, "wait")
            c = first[r, :, ends : ends + Q]
            decay = first[r, :, ends + Q :]
            for at in range(0, done.shape[2], step):
                head = iota((Q, step), 0)
                pick = jnp.where(head == (iota((Q, step), 1) + at) // HDIM, 1.0, 0.0).astype(BF)
                add = dot(decay, pick) * dot(c, enter[r, :, at : at + step])
                here = first[r, :, at : at + step] if at < ends else other[r, :, at - ends : at - ends + step]
                done[r, :, at : at + step] = (here.astype(F32) + add).astype(BF)

        write_owned(plan, r, done.at[r], out, lanes, s_out)
    for r, plan in enumerate(plans):
        write_owned(plan, r, done.at[r], out, lanes, s_out, None, "wait")
        write_owned(plan, r, None, out, pl.ds(0, zeros.shape[1]), s_zero, zeros, "wait")


def owned_kernel(start, which, owner, *refs):
    out, held, s_in, s_out = refs[-4:]
    plans = owned_plan(owner, 4)
    width = refs[0].shape[1]
    half = out.shape[2] // CORES
    lane = (CORES - 1 - core_at()) * half + start * HDIM
    lanes = pl.ds(pl.multiple_of(lane, GH * HDIM), width)
    if isinstance(which, int):
        for act in ("start", "wait"):
            write_owned(plans[which], which, refs[0], out, lanes, s_out, None, act)
        return
    sources = dict(zip(which, refs))
    for act in ("start", "wait"):
        for r in which:
            plan = plans[r]

            @pl.when(jnp.logical_or(plan[1], plan[2]))
            def _():
                read_part(sources, r, held, s_in, act)

            if act == "wait":
                write_owned(plan, r, held.at[r], out, lanes, s_out)
    for r in which:
        write_owned(plans[r], r, held.at[r], out, lanes, s_out, None, "wait")


def inside(shape):
    return pltpu.VMEM(shape.shape, shape.dtype)


def near(arrays):
    return [pltpu.with_memory_space_constraint(x, pltpu.VMEM) for x in arrays]


def far(arrays):
    return [pltpu.with_memory_space_constraint(x, pltpu.HBM) for x in arrays]


def whole(values, b_in, c_in, log_decay, skip, owner):
    seq_n = lax.axis_size("seq")
    doc_n = lax.axis_size("doc")
    per_level = ROW * CORES
    levels = seq_n // per_level
    values, b_in, c_in, log_decay = values[0], b_in[0], c_in[0], log_decay[0]
    tokens, width = values.shape
    heads = log_decay.shape[0]
    n = b_in.shape[1]

    def shifted(x, step_x=0, step_z=0, swap=0):
        pairs = []
        for i in range(seq_n):
            z, at, core = i // per_level, i % per_level // CORES, i % CORES
            z, at, core = (z + step_z) % levels, (at + step_x) % ROW, (core + swap) % CORES
            pairs.append((i, z * per_level + at * CORES + core))
        return lax.ppermute(x, "seq", pairs)

    def along_row(pieces):
        return [pieces[0]] + [shifted(pieces[k], step_x=k) for k in range(1, ROW)]

    def over_docs(x, k):
        return lax.ppermute(x, "doc", [(d, (d + k) % doc_n) for d in range(doc_n)])

    def over_all_docs(x, far_by):
        before = over_docs(x, 1)
        after = over_docs(x, doc_n - 1)
        far = over_docs(before, 1) if far_by > 0 else over_docs(after, doc_n - 1)
        return [x, after, far, before]

    smem = pl.BlockSpec(memory_space=pltpu.SMEM)
    vmem = pl.BlockSpec(memory_space=pltpu.VMEM)
    anywhere = pl.BlockSpec(memory_space=pl.ANY)

    first_width = EARLY[0] * HDIM
    dma = pltpu.SemaphoreType.DMA

    def local_scratch(count, small=3):
        return [
            pltpu.VMEM((tokens, count * HDIM), BF),
            pltpu.VMEM((heads, tokens), F32),
            pltpu.VMEM((tokens, n), BF),
            pltpu.VMEM((tokens, n), BF),
            pltpu.VMEM((tokens, tokens), BF),
            pltpu.VMEM((tokens, tokens), F32),
            dma((small + count // GH,)),
        ]

    first = pl.pallas_call(
        first_local_kernel,
        name="local_first",
        out_shape=jax.ShapeDtypeStruct((tokens, first_width + 2 * Q), BF),
        in_specs=[smem] + [anywhere] * 4,
        out_specs=vmem,
        scratch_shapes=local_scratch(EARLY[0]),
    )(skip, values, log_decay, b_in, c_in)
    firsts = over_all_docs(first, -1)

    half = width // CORES
    pw = half // ROW
    half_shape = jax.ShapeDtypeStruct((n + TAIL, half), BF)
    piece = jax.ShapeDtypeStruct((n + TAIL, pw), BF)
    mine, other_half = pl.pallas_call(
        states_kernel,
        name="states",
        out_shape=[inside(half_shape)] * 2,
        in_specs=[anywhere] * 3,
        out_specs=[vmem] * 2,
        scratch_shapes=[
            pltpu.VMEM((tokens, width), BF),
            pltpu.VMEM((heads, tokens), F32),
            pltpu.VMEM((tokens, n), BF),
            pltpu.VMEM((4 * WIDE // HDIM, WIDE), BF),
            pltpu.VMEM((CORES,) + half_shape.shape, BF),
            dma((2 + width // WIDE,)),
        ],
    )(values, log_decay, b_in)
    theirs = shifted(other_half, swap=1)
    *pieces, earlier = pl.pallas_call(
        chip_kernel,
        name="chip",
        out_shape=[inside(piece)] * ROW + [inside(half_shape)],
        in_specs=[vmem, vmem],
        out_specs=[vmem] * (ROW + 1),
        scratch_shapes=[pltpu.VMEM((ROW,) + piece.shape, BF)],
    )(*near([mine, theirs]))
    pieces = along_row(pieces)

    other = pl.pallas_call(
        functools.partial(other_local_kernel, EARLY[0]),
        name="local_other",
        out_shape=pltpu.VMEM((tokens, EARLY[1] * HDIM), BF),
        in_specs=[smem] + [anywhere] * 4,
        out_specs=vmem,
        scratch_shapes=local_scratch(EARLY[1]),
    )(skip, values, log_decay, b_in, c_in)
    others = over_all_docs(other, 1)

    row = pl.pallas_call(
        row_kernel, name="row", out_shape=inside(piece), in_specs=[vmem] * ROW, out_specs=vmem
    )(*near(pieces))
    rows = [shifted(row, step_z=k) for k in (1, 2, 3)]
    enter = jax.ShapeDtypeStruct((n, pw), BF)
    enters = pl.pallas_call(
        enter_kernel,
        name="enter",
        out_shape=[inside(enter)] * ROW,
        in_specs=[vmem] * (ROW + 3),
        out_specs=[vmem] * ROW,
        scratch_shapes=[
            pltpu.VMEM((ROW, n, pw), BF),
            pltpu.VMEM((ROW, 8, pw), F32),
            pltpu.VMEM((ROW, n, pw), BF),
        ],
    )(*near(pieces + rows))
    enters = along_row(enters)
    keep, give = pl.pallas_call(
        split_kernel,
        name="split",
        out_shape=[pltpu.VMEM((n, half), BF)] * 2,
        in_specs=[vmem] * (ROW + 1),
        out_specs=[vmem] * 2,
        scratch_shapes=[pltpu.VMEM((ROW, n, pw), BF)],
    )(*near([earlier] + enters))
    got = shifted(give, swap=1)
    early_enters = over_all_docs(keep, -1)

    lates = []
    start = 0
    for i, count in enumerate(LATE):
        late = pl.pallas_call(
            functools.partial(late_kernel, start),
            out_shape=pltpu.VMEM((tokens, count * HDIM), BF),
            in_specs=[smem, vmem] + [anywhere] * 4,
            out_specs=vmem,
            scratch_shapes=local_scratch(count),
        )(skip, *near([got]), values, log_decay, b_in, c_in)
        lates.append((start, over_all_docs(late, 1 if i == 0 else -1)))
        start += count

    result = jax.ShapeDtypeStruct((doc_n * 2, Q, width), BF)
    owned = pl.pallas_call(
        finish_kernel,
        name="finish",
        out_shape=result,
        in_specs=[smem] + [anywhere] * 12,
        out_specs=anywhere,
        scratch_shapes=[
            pltpu.VMEM((doc_n,) + first.shape, BF),
            pltpu.VMEM((doc_n,) + other.shape, BF),
            pltpu.VMEM((doc_n,) + keep.shape, BF),
            pltpu.VMEM((doc_n, tokens, half), BF),
            pltpu.VMEM((Q, width), BF),
            dma((doc_n,)),
            dma((doc_n,)),
            dma((doc_n,)),
            dma((doc_n * 2,)),
            dma((doc_n * 2,)),
        ],
    )(owner, *far(firsts), *far(others), *far(early_enters))

    def write_late(owned, i, which):
        start, arrays = lates[i]
        if isinstance(which, int):
            arrays = near([arrays[which]])
        else:
            arrays = far([arrays[r] for r in which])
        return pl.pallas_call(
            functools.partial(owned_kernel, start, which),
            out_shape=result,
            in_specs=[smem] + [vmem if len(arrays) == 1 else anywhere] * len(arrays) + [anywhere],
            out_specs=anywhere,
            scratch_shapes=[
                pltpu.VMEM((doc_n,) + arrays[0].shape, BF),
                dma((doc_n,)),
                dma((doc_n * 2,)),
            ],
            input_output_aliases={1 + len(arrays): 0},
        )(owner, *arrays, owned)

    near_docs, far_doc = (0, 1, 3), 2
    for i in (1, 0):
        owned = write_late(owned, i, near_docs)
    for i in (1, 0):
        owned = write_late(owned, i, far_doc)
    return owned[None]


def solution(mesh):
    in_specs = (
        P("doc", "seq", None),
        P("doc", "seq", None),
        P("doc", "seq", None),
        P("doc", None, "seq"),
        P(),
        P(None, "seq"),
    )
    out_specs = P("doc", "seq", None, None)
    return jax.shard_map(whole, mesh=mesh, in_specs=in_specs, out_specs=out_specs, check_vma=False)
```
